512 devices in a mesh: kpt: 8 (over x, core), band: 64 (over y, z).
Axes of the slice: x: 4, y: 8, z: 8, core: 2. Of those that a mesh axis runs over, the one named last changes fastest.
Arguments:
- orbitals: bfloat16 [8, 2, 256, 32768], P('kpt', None, 'band'), may hold values from -6 to 6
- potential: float32 [32768], replicated, may hold values from -3 to -0.5
- kernel: float32 [8, 32768], P('kpt'), may hold values from 0.1 to 4
- owners: int32 [4], replicated, may hold values from 0 to 255, as said below
- partner: int32 [8, 4], replicated, may hold values from 0 to 7, as said below
Outputs:
- residual: bfloat16 [8, 2, 256, 32768], P('kpt', None, 'band')
The draws below stay inside these ranges and needn't reach their ends.
Inputs may be any that keep to these rules, and one draw needn't show every extreme that they name: `owners`: 4 distinct band indices, among them 0 and 255. `partner`: k-point indices.
All inputs are finite; a program needn't handle non-finite values.
Results may differ from the reference program's by a relative error of at most 0.0075.
Values may be sent and summed in bfloat16 or wider, within the bound.
A program may use at most 128 MiB of HBM per device.

```python
import math
import jax
import jax.numpy as jnp
from jax import lax

G = 32
GRID = 32768
BANDS = 256
OWNERS = 4
NK = 8


def draw_owners(key, part):
    middle = 1 + jax.random.permutation(key, BANDS - 2)[:OWNERS - 2]
    chosen = jnp.concatenate([jnp.zeros((1,), jnp.int32), middle.astype(jnp.int32), jnp.full((1,), BANDS - 1, jnp.int32)])
    return jax.random.permutation(jax.random.fold_in(key, 7), chosen)


def draw_partner(key, part):
    drawn = jax.random.randint(jax.random.fold_in(key, 11), (NK * OWNERS,), 0, NK, dtype=jnp.int32)
    position = jnp.arange(NK * OWNERS, dtype=jnp.int32)
    drawn = jnp.where(position == 0, NK - 1, drawn)
    drawn = jnp.where(position == NK * OWNERS - 1, 0, drawn)
    return drawn.reshape(NK, OWNERS)


def with_spikes(values, rng, source, target, parts, factor):
    owner, partner = [(jnp.arange(values.shape[dim]) // (values.shape[dim] // parts)).reshape([-1 if axis == dim else 1 for axis in range(values.ndim)]) for dim in (source, target)]
    chosen = jax.random.permutation(rng, parts)[partner]
    strong = (owner == chosen) | (owner == (partner + parts // 2) % parts)
    return jnp.where(strong, factor * values, values)


def levels(own_key, extent, shards, low, high):
    def one(dim, shards_of):
        steps = jax.random.uniform(jax.random.fold_in(jax.random.fold_in(own_key, 6), dim), (shards_of,), jnp.float32, low / len(shards), high / len(shards))
        return jnp.repeat(jnp.exp(steps), extent[dim] // shards_of).reshape((-1,) + (1,) * (len(extent) - dim - 1))

    gain = one(*shards[0])
    for cut in shards[1:]:
        gain = gain * one(*cut)
    return gain


def heavy_noise(key, shape, spread, bound, shards, heavy, held_as=jnp.bfloat16):
    values = spread * jax.random.normal(key, shape, jnp.float32)
    if shards:
        values = values * levels(key, shape, shards, -0.22, 0.18)
    return jnp.clip(with_spikes(values, jax.random.fold_in(key, 3), *heavy), -bound, bound).astype(held_as)


def setup_inputs(seed: int = 0) -> dict:
    arg_keys = jax.random.split(jax.random.key(seed), 6)
    orbitals = heavy_noise(arg_keys[0], (NK, 2, BANDS, GRID), 0.7071, 6.0, ((0, 8), (2, 64)), (3, 2, 64, 4.0))
    potential = jnp.clip(jax.random.uniform(arg_keys[1], (GRID,), jnp.float32, -3.0, -0.5), -3.0, -0.5)
    kernel = jnp.clip(jnp.exp(math.log(4.0) - 3.6888794 * jax.random.uniform(arg_keys[2], (NK, GRID), jnp.float32) ** levels(arg_keys[2], (NK, GRID), ((0, 8),), -0.2, 0.2)), 0.1, 4.0)
    owners = draw_owners(jax.random.fold_in(arg_keys[5], 71), 0)
    partner = draw_partner(jax.random.fold_in(arg_keys[5], 71), 0)
    return dict(orbitals=orbitals, potential=potential, kernel=kernel, owners=owners, partner=partner)


FRACTION = 0.25
HIGHEST = lax.Precision.HIGHEST


def exchange_band(orbital, phases, kernel_grid):
    band_re = orbital[0].astype(jnp.float32)
    band_im = orbital[1].astype(jnp.float32)
    owner_re = phases[:, 0].astype(jnp.float32)
    owner_im = phases[:, 1].astype(jnp.float32)
    density = lax.complex(owner_re * band_re + owner_im * band_im, owner_re * band_im - owner_im * band_re)
    cubes = density.reshape(-1, G, G, G)
    spectrum = jnp.fft.fftn(cubes, axes=(1, 2, 3)) * kernel_grid.reshape(G, G, G)
    solved = jnp.fft.ifftn(spectrum, axes=(1, 2, 3)).reshape(-1, GRID)
    solved_re = jnp.real(solved)
    solved_im = jnp.imag(solved)
    term_re = jnp.sum(owner_re * solved_re - owner_im * solved_im, axis=0)
    term_im = jnp.sum(owner_re * solved_im + owner_im * solved_re, axis=0)
    return -FRACTION * jnp.stack([term_re, term_im])


def combine(over_re, over_im, rows_re, rows_im, proj_re, proj_im):
    mixed_re = jnp.dot(over_re, proj_re, precision=HIGHEST) - jnp.dot(over_im, proj_im, precision=HIGHEST)
    mixed_im = jnp.dot(over_re, proj_im, precision=HIGHEST) + jnp.dot(over_im, proj_re, precision=HIGHEST)
    return jnp.stack([2.0 * rows_re - mixed_re, 2.0 * rows_im - mixed_im])


def build_block(coeff):
    real_t = coeff[0].T
    imag_t = coeff[1].T
    upper = jnp.concatenate([real_t, -imag_t], axis=1)
    lower = jnp.concatenate([imag_t, real_t], axis=1)
    return jnp.concatenate([upper, lower], axis=0)


def project(kpoint_orbitals, values):
    orbit_wide = kpoint_orbitals.astype(jnp.float32)
    value_wide = values.astype(jnp.float32)
    cross_own = jnp.einsum("cig,djg->cidj", orbit_wide, orbit_wide, precision=HIGHEST) / GRID
    cross_val = jnp.einsum("cig,djg->cidj", orbit_wide, value_wide, precision=HIGHEST) / GRID
    over_re = cross_own[0, :, 0] + cross_own[1, :, 1]
    over_im = cross_own[0, :, 1] - cross_own[1, :, 0]
    proj_re = cross_val[0, :, 0] + cross_val[1, :, 1]
    proj_im = cross_val[0, :, 1] - cross_val[1, :, 0]
    coeff = combine(over_re, over_im, proj_re, proj_im, proj_re, proj_im).astype(jnp.bfloat16)
    mixing = build_block(coeff)
    correction = jnp.dot(mixing, kpoint_orbitals.reshape(2 * BANDS, GRID), preferred_element_type=jnp.float32)
    result = value_wide.reshape(2 * BANDS, GRID) - correction
    return result.reshape(2, BANDS, GRID).astype(jnp.bfloat16)


def reference(orbitals, potential, kernel, owners, partner):
    def one_kpoint(kpoint):
        kpoint_orbitals = orbitals[kpoint]
        sources = partner[kpoint].astype(jnp.int32)
        phases = orbitals[sources, :, owners]
        kernel_grid = kernel[kpoint]
        exchange = lax.map(lambda orbital: exchange_band(orbital, phases, kernel_grid), jnp.transpose(kpoint_orbitals, (1, 0, 2)))
        values = (potential * kpoint_orbitals.astype(jnp.float32) + jnp.transpose(exchange, (1, 0, 2))).astype(jnp.bfloat16)
        return project(kpoint_orbitals, values)

    return lax.map(one_kpoint, jnp.arange(NK, dtype=jnp.int32))
```

```python
import functools

import jax
import jax.numpy as jnp
import numpy as np
from jax import lax
from jax.experimental import pallas as pl
from jax.experimental.pallas import tpu as pltpu
from jax.sharding import PartitionSpec as P

GRID = 32768
OWNERS = 4
SHARE = -0.25
SCALE = 1.6245
MESH = pl.DeviceIdType.MESH
F32 = jnp.float32
BF16 = jnp.bfloat16


def as_real(m):
    return np.block([[m.real, -m.imag], [m.imag, m.real]])


def tables():
    spot = np.arange(256)
    plane = (spot % 64) * 4 + spot // 64
    cell_x, cell_y = plane // 8, plane % 8
    freq_x, freq_y = spot % 32, spot // 32
    outer = np.exp(
        -2j * np.pi * (freq_x[:, None] * cell_x / 32 + freq_y[:, None] * cell_y / 8)
    )
    lane = np.arange(128)
    high, last = lane // 32, lane % 32
    inner = [
        np.exp(
            -2j
            * np.pi
            * ((h + 8 * high[:, None]) * high / 32 + last[:, None] * last / 32)
        )
        for h in range(8)
    ]
    first = (SCALE * as_real(outer)).astype(BF16)
    second = np.stack([(SCALE * as_real(m).T) for m in inner]).astype(BF16)
    return first, np.ascontiguousarray(first.T), second


def far_first(step):
    def offset(j):
        return 4 + ((j + 1) // 2) * (1 - 2 * (j % 2))

    return offset(step // 8), offset(step % 8)


def kernel(
    x, pot, kern, owners, partner, first_hbm, firstt_hbm, second_hbm,
    out,
    first, firstt, second, spread, bands, kgrid,
    osend, orecv, xs, sh, phsend, ph, msend, mrecv, mown, mall, mt,
    dens, mid, acc, vsend, vrecv, ys, psend, precv, cown, call, rsend,
    csem, ssem, rsem,
):
    me = lax.axis_index("band")
    mine = lax.axis_index("kpt")
    row, col = me // 8, me % 8

    def peer(step):
        dy, dz = far_first(step)
        return lax.rem(row + dy, 8) * 8 + lax.rem(col + dz, 8)

    barrier = pltpu.get_barrier_semaphore()

    def greet(step, _):
        pl.semaphore_signal(barrier, inc=1, device_id={"band": peer(step)}, device_id_type=MESH)
        return 0

    lax.fori_loop(0, 63, greet, 0)

    def greet_kpt(step, _):
        pl.semaphore_signal(
            barrier, inc=1, device_id={"kpt": lax.rem(mine + step, 8)}, device_id_type=MESH
        )
        return 0

    lax.fori_loop(1, 8, greet_kpt, 0)

    loads = [
        pltpu.make_async_copy(src, dst, csem.at[i])
        for i, (src, dst) in enumerate(
            ((first_hbm, first), (firstt_hbm, firstt), (second_hbm, second))
        )
    ]
    for load in loads:
        load.start()

    def spread_out(source, dst, which, f):
        for i in range(4):
            dst[which, i * 64 : (i + 1) * 64, :] = source[pl.ds(i * 512 + f, 64, stride=8), :]

    def pack(d, _):
        block = x[:, :, pl.ds(pl.multiple_of(d * 512, 512), 512)]
        wide = block.astype(F32).reshape(8, 512)
        for i in range(4):
            spread[pl.ds(pl.multiple_of(d * 8, 8) + i * 512, 8), :] = wide[:, i * 128 : (i + 1) * 128]
        osend[d] = wide.astype(BF16)
        return 0

    lax.fori_loop(0, 64, pack, 0)

    pl.semaphore_wait(barrier, 70)

    def to_all(n, source, dst):
        def go(step, _):
            p = peer(step)
            pltpu.make_async_remote_copy(
                src_ref=source(p),
                dst_ref=dst.at[me],
                send_sem=ssem.at[n],
                recv_sem=rsem.at[n],
                device_id={"band": p},
                device_id_type=MESH,
            ).start()
            return 0

        lax.fori_loop(0, 63, go, 0)

    def arrived(n, dst):
        part = dst.at[pl.ds(0, 63)]
        pltpu.make_async_copy(part, part, rsem.at[n]).wait()

    def left(n, dst):
        part = dst.at[pl.ds(0, 63)]
        pltpu.make_async_copy(part, part, ssem.at[n]).wait()

    orecv[me] = osend[me]
    to_all(0, lambda p: osend.at[p], orecv)

    for f in range(8):
        spread_out(spread, bands, f, f)
    lane128 = lax.broadcasted_iota(jnp.int32, (32, 128), 1)
    for h in range(8):
        tile = jnp.zeros((32, 128), F32)
        for j in range(4):
            piece = kern[pl.ds(2 * j + h // 4, 32, stride=8), :]
            shift = (j * 32 - (h % 4) * 32) % 128
            if shift:
                piece = pltpu.roll(piece, shift, 1)
            tile = jnp.where(lane128 // 32 == j, piece, tile)
        kgrid[h] = tile * (1.0 / (GRID * SCALE**4))

    arrived(0, orecv)
    xs[...] = orecv[...].astype(F32).reshape(512, 512).astype(BF16)

    line = lax.broadcasted_iota(jnp.int32, (8, 512), 0)
    place = lax.broadcasted_iota(jnp.int32, (8, 512), 1)
    want = jnp.zeros((8, 512), jnp.int32)
    for o in range(OWNERS):
        band = owners[o]
        base = (band // 4) * 8 + band % 4
        want = jnp.where(line // 2 == o, base + (line % 2) * 4, want)
    pick = jnp.where(place == want, 1.0, 0.0).astype(BF16)
    share = jnp.dot(pick, xs[...], preferred_element_type=F32).astype(BF16)
    sh[mine] = share

    def kpt_copy(step):
        return pltpu.make_async_remote_copy(
            src_ref=sh.at[mine],
            dst_ref=sh.at[mine],
            send_sem=ssem.at[8],
            recv_sem=rsem.at[8],
            device_id={"kpt": lax.rem(mine + step, 8)},
            device_id_type=MESH,
        )

    def kpt_go(step, _):
        kpt_copy(step).start()
        return 0

    lax.fori_loop(1, 8, kpt_go, 0)

    group = lax.broadcasted_iota(jnp.int32, (512, 512), 1) % 8 < 4

    def fold(gram):
        low = pltpu.roll(gram, 508, 0)
        swapped = jnp.where(group, pltpu.roll(low, 508, 1), -pltpu.roll(low, 4, 1))
        return ((gram + swapped) * (1.0 / GRID)).reshape(64, 8, 512)[:, :4, :]

    def widen(rows):
        flat = rows.reshape(256, 512)
        other = jnp.where(group[:256], -pltpu.roll(flat, 508, 1), pltpu.roll(flat, 4, 1))
        return jnp.concatenate([rows, other.reshape(64, 4, 512)], axis=1).reshape(512, 512)

    def gram_of(left_ref):
        return lax.dot_general(
            left_ref[...], xs[...], (((1,), (1,)), ((), ())), preferred_element_type=F32
        )

    msend[...] = fold(gram_of(xs)).astype(BF16)

    part7 = sh.at[pl.ds(0, 7)]
    pltpu.make_async_copy(part7, part7, rsem.at[8]).wait()
    wanted = jnp.zeros((8, 512), jnp.int32)
    for o in range(OWNERS):
        wanted = jnp.where(line // 2 == o, partner[mine, o], wanted)
    got = jnp.zeros((8, 512), F32)
    for k in range(8):
        got = jnp.where(wanted == k, sh[k].astype(F32), got)
    phsend[...] = got.astype(BF16)
    ph[me] = phsend[...]
    to_all(1, lambda p: phsend, ph)

    mrecv[me] = msend[me]
    to_all(2, lambda p: msend.at[p], mrecv)

    arrived(1, ph)
    for load in loads:
        load.wait()
    for i in range(4):
        at = slice(i * 128, (i + 1) * 128)
        spread[i * 512 : (i + 1) * 512, :] = ph[:, :, at].astype(F32).reshape(512, 128)

    def phase(f):
        return jnp.concatenate(
            [spread[pl.ds(i * 512 + f, 64, stride=8), :] for i in range(4)], axis=0
        )

    for o in range(OWNERS):
        ph_re, ph_im = phase(2 * o), phase(2 * o + 1)
        for b in range(4):
            b_re, b_im = bands[b], bands[4 + b]
            at = b * 128
            dens[0:256, at : at + 128] = (ph_re * b_re + ph_im * b_im).astype(BF16)
            dens[256:512, at : at + 128] = (ph_re * b_im - ph_im * b_re).astype(BF16)
        mid[:, o * 512 : (o + 1) * 512] = jnp.dot(
            first[...], dens[...], preferred_element_type=F32
        ).astype(BF16)

    arrived(2, mrecv)
    mown[...] = jnp.sum(mrecv[...].astype(F32), axis=0)
    mall[me] = mown[...]
    to_all(3, lambda p: mown, mall)

    def inner(h, _):
        r = pl.multiple_of(h * 32, 32)
        rows = jnp.concatenate(
            [
                jnp.concatenate(
                    [
                        mid[pl.ds(r + 256 * c, 32), f * 128 : (f + 1) * 128]
                        for c in range(2)
                    ],
                    axis=1,
                )
                for f in range(16)
            ],
            axis=0,
        )
        spectrum = jnp.dot(rows, second[h], preferred_element_type=F32)
        factor = jnp.concatenate([kgrid[h], kgrid[h]], axis=1)
        spectrum = (spectrum.reshape(16, 32, 256) * factor[None]).reshape(512, 256).astype(BF16)
        back = lax.dot_general(
            spectrum, second[h], (((1,), (1,)), ((), ())), preferred_element_type=F32
        ).astype(BF16)
        for f in range(16):
            for c in range(2):
                mid[pl.ds(r + 256 * c, 32), f * 128 : (f + 1) * 128] = back[
                    f * 32 : (f + 1) * 32, c * 128 : (c + 1) * 128
                ]
        return 0

    lax.fori_loop(0, 8, inner, 0)

    for o in range(OWNERS):
        ph_re, ph_im = phase(2 * o), phase(2 * o + 1)
        solved = jnp.dot(
            firstt[...], mid[:, o * 512 : (o + 1) * 512], preferred_element_type=F32
        )
        for b in range(4):
            s_re = solved[0:256, b * 128 : (b + 1) * 128]
            s_im = solved[256:512, b * 128 : (b + 1) * 128]
            t_re = ph_re * s_re - ph_im * s_im
            t_im = ph_re * s_im + ph_im * s_re
            if o:
                t_re = acc[b] + t_re
                t_im = acc[4 + b] + t_im
            acc[b] = t_re
            acc[4 + b] = t_im

    for i in range(4):
        local = pot[pl.ds(i, 64, stride=4), :]
        rows = slice(i * 64, (i + 1) * 64)
        for f in range(8):
            spread[pl.ds(i * 512 + f, 64, stride=8), :] = (
                local * bands[f, rows, :] + SHARE * acc[f, rows, :]
            )
    for i in range(4):
        part = spread[i * 512 : (i + 1) * 512, :].reshape(64, 8, 128)
        vsend[:, :, i * 128 : (i + 1) * 128] = part.astype(BF16)
    vrecv[me] = vsend[me]
    to_all(4, lambda p: vsend.at[p], vrecv)

    arrived(3, mall)
    mt[...] = widen(mall[...])

    arrived(4, vrecv)
    wide = vrecv[...].astype(F32).reshape(512, 512)
    ys[...] = wide.astype(BF16)
    psend[...] = fold(gram_of(ys)).astype(BF16)
    precv[me] = psend[me]
    to_all(5, lambda p: psend.at[p], precv)

    arrived(5, precv)
    proj = jnp.sum(precv[...].astype(F32), axis=0)
    coeff = 2.0 * proj - jnp.dot(
        proj, mt[...], precision=lax.Precision.HIGHEST, preferred_element_type=F32
    )
    cown[...] = coeff.astype(BF16)
    call[me] = cown[...]
    to_all(6, lambda p: cown, call)

    arrived(6, call)
    mixing = widen(call[...].astype(F32)).astype(BF16)
    correction = jnp.dot(mixing, xs[...], preferred_element_type=F32)
    rsend[...] = (ys[...].astype(F32) - correction).reshape(64, 8, 512).astype(BF16)
    out[me] = rsend[me]
    to_all(7, lambda p: rsend.at[p], out)
    arrived(7, out)

    left(0, osend)
    left(1, ph)
    left(2, msend)
    left(3, mall)
    left(4, vsend)
    left(5, psend)
    left(6, call)
    left(7, rsend)
    pltpu.make_async_copy(part7, part7, ssem.at[8]).wait()


def unpack(block, out):
    def one(d, _):
        wide = block[d].astype(F32)
        at = pl.ds(pl.multiple_of(d * 512, 512), 512)
        out[:, :, at] = wide.reshape(2, 4, 512).astype(BF16)
        return 0

    lax.fori_loop(0, 64, one, 0)


def body(orbitals, potential, kernel_grid, owners, partner):
    first, firstt, second = tables()
    vmem = pl.BlockSpec(memory_space=pltpu.VMEM)
    smem = pl.BlockSpec(memory_space=pltpu.SMEM)
    anywhere = pl.BlockSpec(memory_space=pl.ANY)
    slab = (64, 8, 512)
    thin = (64, 4, 512)
    block = pl.pallas_call(
        kernel,
        out_shape=jax.ShapeDtypeStruct(slab, BF16),
        in_specs=[vmem, vmem, vmem, smem, smem, anywhere, anywhere, anywhere],
        out_specs=vmem,
        scratch_shapes=[
            pltpu.VMEM((512, 512), BF16),
            pltpu.VMEM((512, 512), BF16),
            pltpu.VMEM((8, 256, 256), BF16),
            pltpu.VMEM((2048, 128), F32),
            pltpu.VMEM((8, 256, 128), F32),
            pltpu.VMEM((8, 32, 128), F32),
            pltpu.VMEM(slab, BF16),
            pltpu.VMEM(slab, BF16),
            pltpu.VMEM((512, 512), BF16),
            pltpu.VMEM((8, 8, 512), BF16),
            pltpu.VMEM((8, 512), BF16),
            pltpu.VMEM(slab, BF16),
            pltpu.VMEM(thin, BF16),
            pltpu.VMEM(thin, BF16),
            pltpu.VMEM((4, 512), F32),
            pltpu.VMEM(thin, F32),
            pltpu.VMEM((512, 512), F32),
            pltpu.VMEM((512, 512), BF16),
            pltpu.VMEM((512, 2048), BF16),
            pltpu.VMEM((8, 256, 128), F32),
            pltpu.VMEM(slab, BF16),
            pltpu.VMEM(slab, BF16),
            pltpu.VMEM((512, 512), BF16),
            pltpu.VMEM(thin, BF16),
            pltpu.VMEM(thin, BF16),
            pltpu.VMEM((4, 512), BF16),
            pltpu.VMEM(thin, BF16),
            pltpu.VMEM(slab, BF16),
            pltpu.SemaphoreType.DMA((3,)),
            pltpu.SemaphoreType.DMA((9,)),
            pltpu.SemaphoreType.DMA((9,)),
        ],
        compiler_params=pltpu.CompilerParams(
            collective_id=0, has_side_effects=True, vmem_limit_bytes=60 << 20
        ),
        name="exchange_residual",
    )(
        orbitals[0],
        potential.reshape(256, 128),
        kernel_grid.reshape(256, 128),
        owners,
        partner,
        first,
        firstt,
        second,
    )
    out = pl.pallas_call(
        unpack,
        out_shape=jax.ShapeDtypeStruct((2, 4, GRID), BF16),
        in_specs=[vmem],
        out_specs=vmem,
        name="unpack",
    )(block)
    return out[None]


def solution(mesh):
    in_specs = (P("kpt", None, "band", None), P(), P("kpt", None), P(), P())
    out_specs = P("kpt", None, "band", None)
    return jax.shard_map(body, mesh=mesh, in_specs=in_specs, out_specs=out_specs, check_vma=False)
```

```python
import jax
import jax.numpy as jnp
import numpy as np
from jax import lax
from jax.experimental import pallas as pl
from jax.experimental.pallas import tpu as pltpu
from jax.sharding import PartitionSpec as P

GRID = 32768
OWNERS = 4
SHARE = -0.25
SCALE = 1.6245
MESH = pl.DeviceIdType.MESH
F32 = jnp.float32
BF16 = jnp.bfloat16


def as_real(m):
    return np.block([[m.real, -m.imag], [m.imag, m.real]])


def tables():
    spot = np.arange(256)
    plane = (spot % 64) * 4 + spot // 64
    cell_x, cell_y = plane // 8, plane % 8
    freq_x, freq_y = spot % 32, spot // 32
    outer = np.exp(
        -2j * np.pi * (freq_x[:, None] * cell_x / 32 + freq_y[:, None] * cell_y / 8)
    )
    lane = np.arange(128)
    high, last = lane // 32, lane % 32
    inner = [
        np.exp(
            -2j
            * np.pi
            * ((h + 8 * high[:, None]) * high / 32 + last[:, None] * last / 32)
        )
        for h in range(8)
    ]
    first = (SCALE * as_real(outer)).astype(BF16)
    second = np.stack([(SCALE * as_real(m).T) for m in inner]).astype(BF16)
    return first, np.ascontiguousarray(first.T), second


def offset(j):
    return 4 + ((j + 1) // 2) * (1 - 2 * (j % 2))


def kernel(
    x_hbm, pot_hbm, kern_hbm, owners, partner, first_hbm, firstt_hbm, second_hbm,
    out,
    x, pot, kern, first, firstt, second, spread, bands, kgrid,
    osend, orecv, xs, sh, ph_a, ph_b, msend, mrecv, mown, mall, mt,
    dens, mid, acc, vsend, vrecv, ys, psend, precv, cown, call, rsend, rrecv, result,
    csem, ssem, rsem, gsem, fsem,
):
    me = lax.axis_index("band")
    mine = lax.axis_index("kpt")
    row, col = me // 8, me % 8

    loads = [
        pltpu.make_async_copy(src, dst, csem.at[i])
        for i, (src, dst) in enumerate(
            (
                (x_hbm, x),
                (pot_hbm, pot),
                (kern_hbm, kern),
                (first_hbm, first),
                (firstt_hbm, firstt),
                (second_hbm, second),
            )
        )
    ]
    for load in loads:
        load.start()

    def around(place, j):
        return lax.rem(place + offset(j), 8)

    barrier = pltpu.get_barrier_semaphore()

    def greet(step, _):
        peer = around(row, step // 8) * 8 + around(col, step % 8)
        pl.semaphore_signal(barrier, inc=1, device_id={"band": peer}, device_id_type=MESH)
        return 0

    lax.fori_loop(0, 63, greet, 0)

    def greet_kpt(step, _):
        pl.semaphore_signal(
            barrier, inc=1, device_id={"kpt": lax.rem(mine + step, 8)}, device_id_type=MESH
        )
        return 0

    lax.fori_loop(1, 8, greet_kpt, 0)

    loads[0].wait()

    def pack(d, _):
        block = x[:, :, pl.ds(pl.multiple_of(d * 512, 512), 512)]
        wide = block.astype(F32).reshape(8, 512)
        for i in range(4):
            spread[pl.ds(pl.multiple_of(d * 8, 8) + i * 512, 8), :] = wide[
                :, i * 128 : (i + 1) * 128
            ]
        osend[d] = wide.astype(BF16)
        return 0

    lax.fori_loop(0, 64, pack, 0)
    pl.semaphore_wait(barrier, 70)

    def send(source, target, peer, n, arrival):
        pltpu.make_async_remote_copy(
            src_ref=source,
            dst_ref=target,
            send_sem=ssem.at[n],
            recv_sem=arrival,
            device_id={"band": peer},
            device_id_type=MESH,
        ).start()

    def wait(sem, dst, count):
        part = dst.at[pl.ds(0, count)]
        pltpu.make_async_copy(part, part, sem).wait()

    def to_all(n, source, dst, arrival):
        def go(step, _):
            peer = around(row, step // 8) * 8 + around(col, step % 8)
            send(source(peer), dst.at[me], peer, n, arrival(step // 8))
            return 0

        lax.fori_loop(0, 63, go, 0)

    def to_row(n, base, count, source, dst, arrival):
        def go(j, _):
            peer = base + around(col, j)
            send(source(peer), dst.at[me], peer, n, arrival)
            return 0

        lax.fori_loop(0, count, go, 0)

    def by_rows(step):
        def run(g, _):
            step(g, 8)
            return 0

        lax.fori_loop(0, 7, run, 0)
        step(7, 7)

    orecv[me] = osend[me]
    to_all(0, lambda p: osend.at[p], orecv, lambda g: rsem.at[0])

    for f in range(8):
        for i in range(4):
            bands[f, i * 64 : (i + 1) * 64, :] = spread[pl.ds(i * 512 + f, 64, stride=8), :]
    loads[2].wait()
    lane128 = lax.broadcasted_iota(jnp.int32, (32, 128), 1)
    for h in range(8):
        tile = jnp.zeros((32, 128), F32)
        for j in range(4):
            piece = kern[pl.ds(2 * j + h // 4, 32, stride=8), :]
            shift = (j * 32 - (h % 4) * 32) % 128
            if shift:
                piece = pltpu.roll(piece, shift, 1)
            tile = jnp.where(lane128 // 32 == j, piece, tile)
        kgrid[h] = tile * (1.0 / (GRID * SCALE**4))

    wait(rsem.at[0], orecv, 63)
    xs[...] = orecv[...].astype(F32).reshape(512, 512).astype(BF16)

    line = lax.broadcasted_iota(jnp.int32, (8, 512), 0)
    place = lax.broadcasted_iota(jnp.int32, (8, 512), 1)
    want = jnp.zeros((8, 512), jnp.int32)
    for o in range(OWNERS):
        band = owners[o]
        base = (band // 4) * 8 + band % 4
        want = jnp.where(line // 2 == o, base + (line % 2) * 4, want)
    pick = jnp.where(place == want, 1.0, 0.0).astype(BF16)
    share = jnp.dot(pick, xs[...], preferred_element_type=F32).astype(BF16)
    sh[mine] = share

    def kpt_go(step, _):
        pltpu.make_async_remote_copy(
            src_ref=sh.at[mine],
            dst_ref=sh.at[mine],
            send_sem=ssem.at[1],
            recv_sem=rsem.at[1],
            device_id={"kpt": lax.rem(mine + step, 8)},
            device_id_type=MESH,
        ).start()
        return 0

    lax.fori_loop(1, 8, kpt_go, 0)

    def fold(gram):
        rows = gram.shape[0]
        half = lax.broadcasted_iota(jnp.int32, gram.shape, 1) % 8 < 4
        low = pltpu.roll(gram, rows - 4, 0)
        swapped = jnp.where(half, pltpu.roll(low, 508, 1), -pltpu.roll(low, 4, 1))
        sums = ((gram + swapped) * (1.0 / GRID)).reshape(rows // 8, 8, 512)[:, :4, :]
        return sums.reshape(rows // 2, 512)

    def widen(flat):
        half = lax.broadcasted_iota(jnp.int32, flat.shape, 1) % 8 < 4
        other = jnp.where(half, -pltpu.roll(flat, 508, 1), pltpu.roll(flat, 4, 1))
        count = flat.shape[0] // 4
        both = [flat.reshape(count, 4, 512), other.reshape(count, 4, 512)]
        return jnp.concatenate(both, axis=1).reshape(count * 8, 512)

    def ahead(shape, base):
        line = lax.broadcasted_iota(jnp.int32, shape, 0)
        lane = lax.broadcasted_iota(jnp.int32, shape, 1)
        return lane - (base + line // 4) * 8 - line % 4

    def halve(flat, base):
        high = flat.astype(BF16).astype(F32)
        rest = pltpu.roll(flat - high, 4, 1)
        return jnp.where(ahead(flat.shape, base) == 4, rest, high).astype(BF16)

    def join(flat, base):
        at = ahead(flat.shape, base)
        whole = flat + pltpu.roll(flat, 508, 1)
        return jnp.where(at == 0, whole, jnp.where(at == 4, 0.0, flat))

    def gram_of(rows):
        return lax.dot_general(
            rows, xs[...], (((1,), (1,)), ((), ())), preferred_element_type=F32
        )

    msend[...] = halve(fold(gram_of(xs[...])), 0).reshape(64, 4, 512)

    wait(rsem.at[1], sh, 7)
    wanted = jnp.zeros((8, 512), jnp.int32)
    for o in range(OWNERS):
        wanted = jnp.where(line // 2 == o, partner[o, mine], wanted)
    got = jnp.zeros((8, 512), F32)
    for k in range(8):
        got = jnp.where(wanted == k, sh[k].astype(F32), got)

    turned = col * 8 + row
    ph_a[me] = got[:, :256].astype(BF16)
    ph_b[turned] = got[:, 256:].astype(BF16)

    def spread_one(j, _):
        send(ph_a.at[me], ph_a.at[me], row * 8 + around(col, j), 2, rsem.at[2])
        send(ph_b.at[turned], ph_b.at[turned], around(row, j) * 8 + col, 10, rsem.at[3])
        return 0

    lax.fori_loop(0, 7, spread_one, 0)
    wait(rsem.at[2], ph_a, 7)
    wait(rsem.at[3], ph_b, 7)

    def spread_all(j, _):
        part_a = ph_a.at[pl.ds(row * 8, 8)]
        part_b = ph_b.at[pl.ds(col * 8, 8)]
        send(part_a, part_a, around(row, j) * 8 + col, 3, rsem.at[4])
        send(part_b, part_b, row * 8 + around(col, j), 11, rsem.at[5])
        return 0

    lax.fori_loop(0, 7, spread_all, 0)

    mrecv[me] = msend[me]
    to_all(4, lambda p: msend.at[p], mrecv, lambda g: rsem.at[6])

    wait(rsem.at[4], ph_a, 56)
    wait(rsem.at[5], ph_b, 56)
    for i in range(4):
        source = ph_a if i < 2 else ph_b
        at = slice((i % 2) * 128, (i % 2 + 1) * 128)
        spread[i * 512 : (i + 1) * 512, :] = source[:, :, at].astype(F32).reshape(512, 128)

    def phase(f):
        parts = [spread[pl.ds(i * 512 + f, 64, stride=8), :] for i in range(2)]
        for i in range(2, 4):
            for r in range(8):
                parts.append(spread[pl.ds(i * 512 + r * 8 + f, 8, stride=64), :])
        return jnp.concatenate(parts, axis=0)

    for load in loads[3:]:
        load.wait()
    for o in range(OWNERS):
        ph_re, ph_im = phase(2 * o), phase(2 * o + 1)
        for b in range(4):
            b_re, b_im = bands[b], bands[4 + b]
            at = b * 128
            dens[0:256, at : at + 128] = (ph_re * b_re + ph_im * b_im).astype(BF16)
            dens[256:512, at : at + 128] = (ph_re * b_im - ph_im * b_re).astype(BF16)
        mid[:, o * 512 : (o + 1) * 512] = jnp.dot(
            first[...], dens[...], preferred_element_type=F32
        ).astype(BF16)

    def inner(h, _):
        r = pl.multiple_of(h * 32, 32)
        rows = jnp.concatenate(
            [
                jnp.concatenate(
                    [
                        mid[pl.ds(r + 256 * c, 32), f * 128 : (f + 1) * 128]
                        for c in range(2)
                    ],
                    axis=1,
                )
                for f in range(16)
            ],
            axis=0,
        )
        spectrum = jnp.dot(rows, second[h], preferred_element_type=F32)
        factor = jnp.concatenate([kgrid[h], kgrid[h]], axis=1)
        spectrum = (spectrum.reshape(16, 32, 256) * factor[None]).reshape(512, 256).astype(BF16)
        back = lax.dot_general(
            spectrum, second[h], (((1,), (1,)), ((), ())), preferred_element_type=F32
        ).astype(BF16)
        for f in range(16):
            for c in range(2):
                mid[pl.ds(r + 256 * c, 32), f * 128 : (f + 1) * 128] = back[
                    f * 32 : (f + 1) * 32, c * 128 : (c + 1) * 128
                ]
        return 0

    lax.fori_loop(0, 8, inner, 0)

    wait(rsem.at[6], mrecv, 63)
    margin = join(jnp.sum(mrecv[...].astype(F32), axis=0), me)
    mown[...] = halve(margin, me)
    mall[me] = mown[...]
    to_all(5, lambda p: mown, mall, lambda g: rsem.at[7])

    for o in range(OWNERS):
        ph_re, ph_im = phase(2 * o), phase(2 * o + 1)
        solved = jnp.dot(
            firstt[...], mid[:, o * 512 : (o + 1) * 512], preferred_element_type=F32
        )
        for b in range(4):
            s_re = solved[0:256, b * 128 : (b + 1) * 128]
            s_im = solved[256:512, b * 128 : (b + 1) * 128]
            t_re = ph_re * s_re - ph_im * s_im
            t_im = ph_re * s_im + ph_im * s_re
            if o:
                t_re = acc[b] + t_re
                t_im = acc[4 + b] + t_im
            acc[b] = t_re
            acc[4 + b] = t_im

    loads[1].wait()
    for i in range(4):
        local = pot[pl.ds(i, 64, stride=4), :]
        rows = slice(i * 64, (i + 1) * 64)
        for f in range(8):
            spread[pl.ds(i * 512 + f, 64, stride=8), :] = (
                local * bands[f, rows, :] + SHARE * acc[f, rows, :]
            )
    for i in range(4):
        part = spread[i * 512 : (i + 1) * 512, :].reshape(64, 8, 128)
        vsend[:, :, i * 128 : (i + 1) * 128] = part.astype(BF16)
    vrecv[me] = vsend[me]
    to_all(6, lambda p: vsend.at[p], vrecv, lambda g: gsem.at[0, g])

    wait(rsem.at[7], mall, 63)
    mt[...] = widen(join(mall[...].astype(F32).reshape(256, 512), 0))

    def take_values(g, count):
        source = lax.rem(row - offset(g) + 8, 8)
        base = pl.multiple_of(source * 8, 8)
        wait(gsem.at[0, g], vrecv, count)
        rows = vrecv[pl.ds(base, 8)].astype(F32).reshape(64, 512).astype(BF16)
        ys[pl.ds(pl.multiple_of(source * 64, 64), 64), :] = rows
        psend[pl.ds(base, 8)] = halve(fold(gram_of(rows)), base).reshape(8, 4, 512)
        to_row(7, base, count, lambda p: psend.at[p], precv, rsem.at[8])

    by_rows(take_values)
    precv[me] = psend[me]
    wait(rsem.at[8], precv, 63)
    proj = join(jnp.sum(precv[...].astype(F32), axis=0), me)
    coeff = 2.0 * proj - jnp.dot(
        proj, mt[...], precision=lax.Precision.HIGHEST, preferred_element_type=F32
    )
    cown[...] = coeff.astype(BF16)
    call[me] = cown[...]
    to_all(8, lambda p: cown, call, lambda g: gsem.at[1, g])

    def take_coefficients(g, count):
        source = lax.rem(row - offset(g) + 8, 8)
        base = pl.multiple_of(source * 8, 8)
        wait(gsem.at[1, g], call, count)
        mixing = widen(call[pl.ds(base, 8)].astype(F32).reshape(32, 512)).astype(BF16)
        correction = jnp.dot(mixing, xs[...], preferred_element_type=F32)
        own = ys[pl.ds(pl.multiple_of(source * 64, 64), 64), :].astype(F32)
        rsend[pl.ds(base, 8)] = (own - correction).reshape(8, 8, 512).astype(BF16)
        to_row(9, base, count, lambda p: rsend.at[p], rrecv, gsem.at[2, g])

    by_rows(take_coefficients)
    rrecv[me] = rsend[me]

    def take_residuals(g, count):
        source = around(row, g)
        wait(gsem.at[2, g], rrecv, count)
        base = pl.multiple_of(source * 4096, 4096)
        for s in range(8):
            wide = rrecv[source * 8 + s].astype(F32).reshape(2, 4, 512)
            result[:, :, pl.ds(base + s * 512, 512)] = wide.astype(BF16)
        cells = pl.ds(base, 4096)
        pltpu.make_async_copy(result.at[:, :, cells], out.at[:, :, cells], fsem).start()

    by_rows(take_residuals)
    pltpu.make_async_copy(result, out, fsem).wait()

    for n, ref in (
        (0, osend), (4, msend), (5, mall), (6, vsend), (7, psend), (8, call), (9, rsend)
    ):
        wait(ssem.at[n], ref, 63)
    wait(ssem.at[1], sh, 7)
    for n, ref in ((2, ph_a), (10, ph_b)):
        wait(ssem.at[n], ref, 7)
    for n, ref in ((3, ph_a), (11, ph_b)):
        wait(ssem.at[n], ref, 56)


def body(orbitals, potential, kernel_grid, owners, partner):
    first, firstt, second = tables()
    smem = pl.BlockSpec(memory_space=pltpu.SMEM)
    anywhere = pl.BlockSpec(memory_space=pl.ANY)
    slab = (64, 8, 512)
    thin = (64, 4, 512)
    out = pl.pallas_call(
        kernel,
        out_shape=jax.ShapeDtypeStruct((2, 4, GRID), BF16),
        in_specs=[anywhere, anywhere, anywhere, smem, smem, anywhere, anywhere, anywhere],
        out_specs=anywhere,
        scratch_shapes=[
            pltpu.VMEM((2, 4, GRID), BF16),
            pltpu.VMEM((256, 128), F32),
            pltpu.VMEM((256, 128), F32),
            pltpu.VMEM((512, 512), BF16),
            pltpu.VMEM((512, 512), BF16),
            pltpu.VMEM((8, 256, 256), BF16),
            pltpu.VMEM((2048, 128), F32),
            pltpu.VMEM((8, 256, 128), F32),
            pltpu.VMEM((8, 32, 128), F32),
            pltpu.VMEM(slab, BF16),
            pltpu.VMEM(slab, BF16),
            pltpu.VMEM((512, 512), BF16),
            pltpu.VMEM((8, 8, 512), BF16),
            pltpu.VMEM((64, 8, 256), BF16),
            pltpu.VMEM((64, 8, 256), BF16),
            pltpu.VMEM(thin, BF16),
            pltpu.VMEM(thin, BF16),
            pltpu.VMEM((4, 512), BF16),
            pltpu.VMEM(thin, BF16),
            pltpu.VMEM((512, 512), F32),
            pltpu.VMEM((512, 512), BF16),
            pltpu.VMEM((512, 2048), BF16),
            pltpu.VMEM((8, 256, 128), F32),
            pltpu.VMEM(slab, BF16),
            pltpu.VMEM(slab, BF16),
            pltpu.VMEM((512, 512), BF16),
            pltpu.VMEM(thin, BF16),
            pltpu.VMEM(thin, BF16),
            pltpu.VMEM((4, 512), BF16),
            pltpu.VMEM(thin, BF16),
            pltpu.VMEM(slab, BF16),
            pltpu.VMEM(slab, BF16),
            pltpu.VMEM((2, 4, GRID), BF16),
            pltpu.SemaphoreType.DMA((6,)),
            pltpu.SemaphoreType.DMA((12,)),
            pltpu.SemaphoreType.DMA((9,)),
            pltpu.SemaphoreType.DMA((3, 8)),
            pltpu.SemaphoreType.DMA,
        ],
        compiler_params=pltpu.CompilerParams(
            collective_id=0, has_side_effects=True, vmem_limit_bytes=60 << 20
        ),
        name="exchange_residual",
    )(
        orbitals[0],
        potential.reshape(256, 128),
        kernel_grid.reshape(256, 128),
        owners,
        partner.T,
        first,
        firstt,
        second,
    )
    return out[None]


def solution(mesh):
    in_specs = (P("kpt", None, "band", None), P(), P("kpt", None), P(), P())
    out_specs = P("kpt", None, "band", None)
    return jax.shard_map(body, mesh=mesh, in_specs=in_specs, out_specs=out_specs, check_vma=False)
```

```python
import jax
import jax.numpy as jnp
import numpy as np
from jax import lax
from jax.experimental import pallas as pl
from jax.experimental.pallas import tpu as pltpu
from jax.sharding import PartitionSpec as P

GRID = 32768
OWNERS = 4
SHARE = -0.25
SCALE = 1.6245
MESH = pl.DeviceIdType.MESH
F32 = jnp.float32
BF16 = jnp.bfloat16


def as_real(m):
    return np.block([[m.real, -m.imag], [m.imag, m.real]])


def tables():
    spot = np.arange(256)
    plane = (spot % 64) * 4 + spot // 64
    cell_x, cell_y = plane // 8, plane % 8
    freq_x, freq_y = spot % 32, spot // 32
    outer = np.exp(
        -2j * np.pi * (freq_x[:, None] * cell_x / 32 + freq_y[:, None] * cell_y / 8)
    )
    lane = np.arange(128)
    high, last = lane // 32, lane % 32
    inner = [
        np.exp(
            -2j
            * np.pi
            * ((h + 8 * high[:, None]) * high / 32 + last[:, None] * last / 32)
        )
        for h in range(8)
    ]
    first = (SCALE * as_real(outer)).astype(BF16)
    second = np.stack([(SCALE * as_real(m).T) for m in inner]).astype(BF16)
    return first, np.ascontiguousarray(first.T), second


def offset(j):
    return 4 + ((j + 1) // 2) * (1 - 2 * (j % 2))


def kernel(
    x_hbm, pot_hbm, kern_hbm, owners, partner, first_hbm, firstt_hbm, second_hbm,
    out,
    x, pot, kern, first, firstt, second, spread, bands, kgrid,
    osend, orecv, xs, sh, ph_a, ph_b, msend, mrecv, m_a, m_b, mall, mt,
    dens, mid, acc, vsend, vrecv, ys, psend, precv, cown, call, rsend, rrecv, result,
    csem, ssem, rsem, gsem, fsem, asem,
):
    me = lax.axis_index("band")
    mine = lax.axis_index("kpt")
    row, col = me // 8, me % 8

    loads = [
        pltpu.make_async_copy(src, dst, csem.at[i])
        for i, (src, dst) in enumerate(
            (
                (x_hbm, x),
                (pot_hbm, pot),
                (kern_hbm, kern),
                (first_hbm, first),
                (firstt_hbm, firstt),
                (second_hbm, second),
            )
        )
    ]
    for load in loads:
        load.start()

    def around(place, j):
        return lax.rem(place + offset(j), 8)

    barrier = pltpu.get_barrier_semaphore()

    def greet(step, _):
        peer = around(row, step // 8) * 8 + around(col, step % 8)
        pl.semaphore_signal(barrier, inc=1, device_id={"band": peer}, device_id_type=MESH)
        return 0

    lax.fori_loop(0, 63, greet, 0)

    def greet_kpt(step, _):
        pl.semaphore_signal(
            barrier, inc=1, device_id={"kpt": lax.rem(mine + step, 8)}, device_id_type=MESH
        )
        return 0

    lax.fori_loop(1, 8, greet_kpt, 0)

    loads[0].wait()

    def pack(d, _):
        block = x[:, :, pl.ds(pl.multiple_of(d * 512, 512), 512)]
        wide = block.astype(F32).reshape(8, 512)
        for i in range(4):
            spread[pl.ds(pl.multiple_of(d * 8, 8) + i * 512, 8), :] = wide[
                :, i * 128 : (i + 1) * 128
            ]
        osend[d] = wide.astype(BF16)
        return 0

    lax.fori_loop(0, 64, pack, 0)
    pl.semaphore_wait(barrier, 70)

    def send(source, target, peer, n, arrival):
        pltpu.make_async_remote_copy(
            src_ref=source,
            dst_ref=target,
            send_sem=ssem.at[n],
            recv_sem=arrival,
            device_id={"band": peer},
            device_id_type=MESH,
        ).start()

    def wait(sem, dst, count):
        part = dst.at[pl.ds(0, count)]
        pltpu.make_async_copy(part, part, sem).wait()

    def to_all(n, source, dst, arrival):
        def go(step, _):
            peer = around(row, step // 8) * 8 + around(col, step % 8)
            send(source(peer), dst.at[me], peer, n, arrival(step // 8))
            return 0

        lax.fori_loop(0, 63, go, 0)

    def to_row(n, base, count, source, dst, arrival):
        def go(j, _):
            peer = base + around(col, j)
            send(source(peer), dst.at[me], peer, n, arrival)
            return 0

        lax.fori_loop(0, count, go, 0)

    def by_rows(step):
        def run(g, _):
            step(g, 8)
            return 0

        lax.fori_loop(0, 7, run, 0)
        step(7, 7)

    def by_near_rows(step):
        def run(i, _):
            step(6 - i, 8)
            return 0

        step(7, 7)
        lax.fori_loop(0, 7, run, 0)

    orecv[me] = osend[me]
    to_all(0, lambda p: osend.at[p], orecv, lambda g: rsem.at[0])

    for f in range(8):
        for i in range(4):
            bands[f, i * 64 : (i + 1) * 64, :] = spread[pl.ds(i * 512 + f, 64, stride=8), :]
    loads[2].wait()
    lane128 = lax.broadcasted_iota(jnp.int32, (32, 128), 1)
    for h in range(8):
        tile = jnp.zeros((32, 128), F32)
        for j in range(4):
            piece = kern[pl.ds(2 * j + h // 4, 32, stride=8), :]
            shift = (j * 32 - (h % 4) * 32) % 128
            if shift:
                piece = pltpu.roll(piece, shift, 1)
            tile = jnp.where(lane128 // 32 == j, piece, tile)
        kgrid[h] = tile * (1.0 / (GRID * SCALE**4))

    wait(rsem.at[0], orecv, 63)
    xs[...] = orecv[...].astype(F32).reshape(512, 512).astype(BF16)

    line = lax.broadcasted_iota(jnp.int32, (8, 512), 0)
    place = lax.broadcasted_iota(jnp.int32, (8, 512), 1)
    want = jnp.zeros((8, 512), jnp.int32)
    for o in range(OWNERS):
        band = owners[o]
        base = (band // 4) * 8 + band % 4
        want = jnp.where(line // 2 == o, base + (line % 2) * 4, want)
    pick = jnp.where(place == want, 1.0, 0.0).astype(BF16)
    share = jnp.dot(pick, xs[...], preferred_element_type=F32).astype(BF16)
    sh[mine] = share

    def kpt_go(step, _):
        pltpu.make_async_remote_copy(
            src_ref=sh.at[mine],
            dst_ref=sh.at[mine],
            send_sem=ssem.at[1],
            recv_sem=rsem.at[1],
            device_id={"kpt": lax.rem(mine + step, 8)},
            device_id_type=MESH,
        ).start()
        return 0

    lax.fori_loop(1, 8, kpt_go, 0)

    def fold(gram):
        rows = gram.shape[0]
        half = lax.broadcasted_iota(jnp.int32, gram.shape, 1) % 8 < 4
        low = pltpu.roll(gram, rows - 4, 0)
        swapped = jnp.where(half, pltpu.roll(low, 508, 1), -pltpu.roll(low, 4, 1))
        sums = ((gram + swapped) * (1.0 / GRID)).reshape(rows // 8, 8, 512)[:, :4, :]
        return sums.reshape(rows // 2, 512)

    def widen(flat):
        half = lax.broadcasted_iota(jnp.int32, flat.shape, 1) % 8 < 4
        other = jnp.where(half, -pltpu.roll(flat, 508, 1), pltpu.roll(flat, 4, 1))
        count = flat.shape[0] // 4
        both = [flat.reshape(count, 4, 512), other.reshape(count, 4, 512)]
        return jnp.concatenate(both, axis=1).reshape(count * 8, 512)

    def ahead(shape, base):
        line = lax.broadcasted_iota(jnp.int32, shape, 0)
        lane = lax.broadcasted_iota(jnp.int32, shape, 1)
        return lane - (base + line // 4) * 8 - line % 4

    def halve(flat, base):
        high = flat.astype(BF16).astype(F32)
        rest = pltpu.roll(flat - high, 4, 1)
        return jnp.where(ahead(flat.shape, base) == 4, rest, high).astype(BF16)

    def join(flat, base):
        at = ahead(flat.shape, base)
        whole = flat + pltpu.roll(flat, 508, 1)
        return jnp.where(at == 0, whole, jnp.where(at == 4, 0.0, flat))

    def gram_of(rows):
        return lax.dot_general(
            rows, xs[...], (((1,), (1,)), ((), ())), preferred_element_type=F32
        )

    msend[...] = halve(fold(gram_of(xs[...])), 0).reshape(64, 4, 512)

    wait(rsem.at[1], sh, 7)
    wanted = jnp.zeros((8, 512), jnp.int32)
    for o in range(OWNERS):
        wanted = jnp.where(line // 2 == o, partner[o, mine], wanted)
    got = jnp.zeros((8, 512), F32)
    for k in range(8):
        got = jnp.where(wanted == k, sh[k].astype(F32), got)

    turned = col * 8 + row
    ph_a[me] = got[:, :256].astype(BF16)
    ph_b[turned] = got[:, 256:].astype(BF16)

    def spread_one(j, _):
        send(ph_a.at[me], ph_a.at[me], row * 8 + around(col, j), 2, asem.at[0, j])
        send(ph_b.at[turned], ph_b.at[turned], around(row, j) * 8 + col, 10, asem.at[1, j])
        return 0

    lax.fori_loop(0, 7, spread_one, 0)

    def pass_on(slot_a, slot_b):
        def go(j, _):
            send(ph_a.at[slot_a], ph_a.at[slot_a], around(row, j) * 8 + col, 3, rsem.at[4])
            send(ph_b.at[slot_b], ph_b.at[slot_b], row * 8 + around(col, j), 11, rsem.at[5])
            return 0

        lax.fori_loop(0, 7, go, 0)

    pass_on(me, turned)

    def relay(i, _):
        j = 6 - i
        wait(asem.at[0, j], ph_a, 1)
        wait(asem.at[1, j], ph_b, 1)
        from_col = lax.rem(col - offset(j) + 8, 8)
        from_row = lax.rem(row - offset(j) + 8, 8)
        pass_on(row * 8 + from_col, col * 8 + from_row)
        return 0

    lax.fori_loop(0, 7, relay, 0)

    mrecv[me] = msend[me]
    to_all(4, lambda p: msend.at[p], mrecv, lambda g: rsem.at[6])

    wait(rsem.at[4], ph_a, 56)
    wait(rsem.at[5], ph_b, 56)
    for i in range(4):
        source = ph_a if i < 2 else ph_b
        at = slice((i % 2) * 128, (i % 2 + 1) * 128)
        spread[i * 512 : (i + 1) * 512, :] = source[:, :, at].astype(F32).reshape(512, 128)

    def phase(f):
        parts = [spread[pl.ds(i * 512 + f, 64, stride=8), :] for i in range(2)]
        for i in range(2, 4):
            for r in range(8):
                parts.append(spread[pl.ds(i * 512 + r * 8 + f, 8, stride=64), :])
        return jnp.concatenate(parts, axis=0)

    for load in loads[3:]:
        load.wait()
    for o in range(OWNERS):
        ph_re, ph_im = phase(2 * o), phase(2 * o + 1)
        for b in range(4):
            b_re, b_im = bands[b], bands[4 + b]
            at = b * 128
            dens[0:256, at : at + 128] = (ph_re * b_re + ph_im * b_im).astype(BF16)
            dens[256:512, at : at + 128] = (ph_re * b_im - ph_im * b_re).astype(BF16)
        mid[:, o * 512 : (o + 1) * 512] = jnp.dot(
            first[...], dens[...], preferred_element_type=F32
        ).astype(BF16)

    def inner(h, _):
        r = pl.multiple_of(h * 32, 32)
        rows = jnp.concatenate(
            [
                jnp.concatenate(
                    [
                        mid[pl.ds(r + 256 * c, 32), f * 128 : (f + 1) * 128]
                        for c in range(2)
                    ],
                    axis=1,
                )
                for f in range(16)
            ],
            axis=0,
        )
        spectrum = jnp.dot(rows, second[h], preferred_element_type=F32)
        factor = jnp.concatenate([kgrid[h], kgrid[h]], axis=1)
        spectrum = (spectrum.reshape(16, 32, 256) * factor[None]).reshape(512, 256).astype(BF16)
        back = lax.dot_general(
            spectrum, second[h], (((1,), (1,)), ((), ())), preferred_element_type=F32
        ).astype(BF16)
        for f in range(16):
            for c in range(2):
                mid[pl.ds(r + 256 * c, 32), f * 128 : (f + 1) * 128] = back[
                    f * 32 : (f + 1) * 32, c * 128 : (c + 1) * 128
                ]
        return 0

    lax.fori_loop(0, 8, inner, 0)

    wait(rsem.at[6], mrecv, 63)
    margin = join(jnp.sum(mrecv[...].astype(F32), axis=0), me)
    whole = halve(margin, me)
    m_a[me] = whole[:, :256]
    m_b[turned] = whole[:, 256:]

    def margin_one(j, _):
        send(m_a.at[me], m_a.at[me], row * 8 + around(col, j), 5, rsem.at[2])
        send(m_b.at[turned], m_b.at[turned], around(row, j) * 8 + col, 12, rsem.at[3])
        return 0

    lax.fori_loop(0, 7, margin_one, 0)

    def margin_all(j, _):
        part_a = m_a.at[pl.ds(row * 8, 8)]
        part_b = m_b.at[pl.ds(col * 8, 8)]
        send(part_a, part_a, around(row, j) * 8 + col, 13, rsem.at[7])
        send(part_b, part_b, row * 8 + around(col, j), 14, rsem.at[9])
        return 0

    for o in range(OWNERS):
        if o == 3:
            wait(rsem.at[2], m_a, 7)
            wait(rsem.at[3], m_b, 7)
            lax.fori_loop(0, 7, margin_all, 0)
        ph_re, ph_im = phase(2 * o), phase(2 * o + 1)
        solved = jnp.dot(
            firstt[...], mid[:, o * 512 : (o + 1) * 512], preferred_element_type=F32
        )
        for b in range(4):
            s_re = solved[0:256, b * 128 : (b + 1) * 128]
            s_im = solved[256:512, b * 128 : (b + 1) * 128]
            t_re = ph_re * s_re - ph_im * s_im
            t_im = ph_re * s_im + ph_im * s_re
            if o:
                t_re = acc[b] + t_re
                t_im = acc[4 + b] + t_im
            acc[b] = t_re
            acc[4 + b] = t_im

    loads[1].wait()
    for i in range(4):
        local = pot[pl.ds(i, 64, stride=4), :]
        rows = slice(i * 64, (i + 1) * 64)
        for f in range(8):
            spread[pl.ds(i * 512 + f, 64, stride=8), :] = (
                local * bands[f, rows, :] + SHARE * acc[f, rows, :]
            )
    for i in range(4):
        part = spread[i * 512 : (i + 1) * 512, :].reshape(64, 8, 128)
        vsend[:, :, i * 128 : (i + 1) * 128] = part.astype(BF16)
    vrecv[me] = vsend[me]
    to_all(6, lambda p: vsend.at[p], vrecv, lambda g: gsem.at[0, g])

    wait(rsem.at[7], m_a, 56)
    wait(rsem.at[9], m_b, 56)

    def gathered(i, _):
        mall[i, :, 0:256] = m_a[i]
        mall[i, :, 256:512] = m_b[lax.rem(i, 8) * 8 + i // 8]
        return 0

    lax.fori_loop(0, 64, gathered, 0)
    mt[...] = widen(join(mall[...].astype(F32).reshape(256, 512), 0))

    def take_values(g, count):
        source = lax.rem(row - offset(g) + 8, 8)
        base = pl.multiple_of(source * 8, 8)
        wait(gsem.at[0, g], vrecv, count)
        rows = vrecv[pl.ds(base, 8)].astype(F32).reshape(64, 512).astype(BF16)
        ys[pl.ds(pl.multiple_of(source * 64, 64), 64), :] = rows
        psend[pl.ds(base, 8)] = halve(fold(gram_of(rows)), base).reshape(8, 4, 512)
        to_row(7, base, count, lambda p: psend.at[p], precv, rsem.at[8])

    by_rows(take_values)
    precv[me] = psend[me]
    wait(rsem.at[8], precv, 63)
    proj = join(jnp.sum(precv[...].astype(F32), axis=0), me)
    coeff = 2.0 * proj - jnp.dot(
        proj, mt[...], precision=lax.Precision.HIGHEST, preferred_element_type=F32
    )
    cown[...] = coeff.astype(BF16)
    call[me] = cown[...]

    def coefficients_out(i, _):
        step = 62 - i
        peer = around(row, step // 8) * 8 + around(col, step % 8)
        send(cown, call.at[me], peer, 8, gsem.at[1, step // 8])
        return 0

    lax.fori_loop(0, 63, coefficients_out, 0)

    def take_coefficients(g, count):
        source = lax.rem(row - offset(g) + 8, 8)
        base = pl.multiple_of(source * 8, 8)
        wait(gsem.at[1, g], call, count)
        mixing = widen(call[pl.ds(base, 8)].astype(F32).reshape(32, 512)).astype(BF16)
        correction = jnp.dot(mixing, xs[...], preferred_element_type=F32)
        own = ys[pl.ds(pl.multiple_of(source * 64, 64), 64), :].astype(F32)
        rsend[pl.ds(base, 8)] = (own - correction).reshape(8, 8, 512).astype(BF16)
        to_row(9, base, count, lambda p: rsend.at[p], rrecv, gsem.at[2, g])

    by_near_rows(take_coefficients)
    rrecv[me] = rsend[me]

    def take_residuals(g, count):
        source = around(row, g)
        wait(gsem.at[2, g], rrecv, count)
        base = pl.multiple_of(source * 4096, 4096)
        for s in range(8):
            wide = rrecv[source * 8 + s].astype(F32).reshape(2, 4, 512)
            result[:, :, pl.ds(base + s * 512, 512)] = wide.astype(BF16)
        cells = pl.ds(base, 4096)
        pltpu.make_async_copy(result.at[:, :, cells], out.at[:, :, cells], fsem).start()

    by_near_rows(take_residuals)
    pltpu.make_async_copy(result, out, fsem).wait()

    for n, ref in (
        (0, osend), (4, msend), (6, vsend), (7, psend), (8, call), (9, rsend)
    ):
        wait(ssem.at[n], ref, 63)
    wait(ssem.at[1], sh, 7)
    for n, ref in ((2, ph_a), (10, ph_b), (5, m_a), (12, m_b)):
        wait(ssem.at[n], ref, 7)
    for n, ref in ((3, ph_a), (11, ph_b), (13, m_a), (14, m_b)):
        wait(ssem.at[n], ref, 56)


def body(orbitals, potential, kernel_grid, owners, partner):
    first, firstt, second = tables()
    smem = pl.BlockSpec(memory_space=pltpu.SMEM)
    anywhere = pl.BlockSpec(memory_space=pl.ANY)
    slab = (64, 8, 512)
    thin = (64, 4, 512)
    out = pl.pallas_call(
        kernel,
        out_shape=jax.ShapeDtypeStruct((2, 4, GRID), BF16),
        in_specs=[anywhere, anywhere, anywhere, smem, smem, anywhere, anywhere, anywhere],
        out_specs=anywhere,
        scratch_shapes=[
            pltpu.VMEM((2, 4, GRID), BF16),
            pltpu.VMEM((256, 128), F32),
            pltpu.VMEM((256, 128), F32),
            pltpu.VMEM((512, 512), BF16),
            pltpu.VMEM((512, 512), BF16),
            pltpu.VMEM((8, 256, 256), BF16),
            pltpu.VMEM((2048, 128), F32),
            pltpu.VMEM((8, 256, 128), F32),
            pltpu.VMEM((8, 32, 128), F32),
            pltpu.VMEM(slab, BF16),
            pltpu.VMEM(slab, BF16),
            pltpu.VMEM((512, 512), BF16),
            pltpu.VMEM((8, 8, 512), BF16),
            pltpu.VMEM((64, 8, 256), BF16),
            pltpu.VMEM((64, 8, 256), BF16),
            pltpu.VMEM(thin, BF16),
            pltpu.VMEM(thin, BF16),
            pltpu.VMEM((64, 4, 256), BF16),
            pltpu.VMEM((64, 4, 256), BF16),
            pltpu.VMEM(thin, BF16),
            pltpu.VMEM((512, 512), F32),
            pltpu.VMEM((512, 512), BF16),
            pltpu.VMEM((512, 2048), BF16),
            pltpu.VMEM((8, 256, 128), F32),
            pltpu.VMEM(slab, BF16),
            pltpu.VMEM(slab, BF16),
            pltpu.VMEM((512, 512), BF16),
            pltpu.VMEM(thin, BF16),
            pltpu.VMEM(thin, BF16),
            pltpu.VMEM((4, 512), BF16),
            pltpu.VMEM(thin, BF16),
            pltpu.VMEM(slab, BF16),
            pltpu.VMEM(slab, BF16),
            pltpu.VMEM((2, 4, GRID), BF16),
            pltpu.SemaphoreType.DMA((6,)),
            pltpu.SemaphoreType.DMA((15,)),
            pltpu.SemaphoreType.DMA((10,)),
            pltpu.SemaphoreType.DMA((3, 8)),
            pltpu.SemaphoreType.DMA,
            pltpu.SemaphoreType.DMA((2, 7)),
        ],
        compiler_params=pltpu.CompilerParams(
            collective_id=0, has_side_effects=True, vmem_limit_bytes=60 << 20
        ),
        name="exchange_residual",
    )(
        orbitals[0],
        potential.reshape(256, 128),
        kernel_grid.reshape(256, 128),
        owners,
        partner.T,
        first,
        firstt,
        second,
    )
    return out[None]


def solution(mesh):
    in_specs = (P("kpt", None, "band", None), P(), P("kpt", None), P(), P())
    out_specs = P("kpt", None, "band", None)
    return jax.shard_map(body, mesh=mesh, in_specs=in_specs, out_specs=out_specs, check_vma=False)
```

```python
import jax
import jax.numpy as jnp
import numpy as np
from jax import lax
from jax.experimental import pallas as pl
from jax.experimental.pallas import tpu as pltpu
from jax.sharding import PartitionSpec as P

GRID = 32768
OWNERS = 4
SHARE = -0.25
SCALE = 1.6245
MESH = pl.DeviceIdType.MESH
F32 = jnp.float32
BF16 = jnp.bfloat16


def as_real(m):
    return np.block([[m.real, -m.imag], [m.imag, m.real]])


def tables():
    spot = np.arange(256)
    plane = (spot // 32 * 8 + spot % 8) * 4 + spot // 8 % 4
    cell_x, cell_y = plane // 8, plane % 8
    freq_x, freq_y = spot % 32, spot // 32
    outer = np.exp(
        -2j * np.pi * (freq_x[:, None] * cell_x / 32 + freq_y[:, None] * cell_y / 8)
    )
    lane = np.arange(128)
    high, last = lane // 32, lane % 32
    inner = [
        np.exp(
            -2j
            * np.pi
            * ((h + 8 * high[:, None]) * high / 32 + last[:, None] * last / 32)
        )
        for h in range(8)
    ]
    first = (SCALE * as_real(outer)).astype(BF16)
    second = np.stack([(SCALE * as_real(m).T) for m in inner]).astype(BF16)
    return first, np.ascontiguousarray(first.T), second


def offset(j):
    return 4 + ((j + 1) // 2) * (1 - 2 * (j % 2))


def kernel(
    x_hbm, pot_hbm, kern_hbm, owners, partner, first_hbm, firstt_hbm, second_hbm,
    out,
    x, pot, kern, first, firstt, second, spread, bands, kgrid,
    osend, orecv, xs, sh, ph_a, ph_b, msend, mrecv, m_a, m_b, mall, mt,
    dens, mid, acc, phases, vsend, vrecv, ys, psend, precv, cown, call, rsend, rrecv, result,
    csem, ssem, rsem, gsem, fsem, asem,
):
    me = lax.axis_index("band")
    mine = lax.axis_index("kpt")
    row, col = me // 8, me % 8

    loads = [
        pltpu.make_async_copy(src, dst, csem.at[i])
        for i, (src, dst) in enumerate(
            (
                (x_hbm, x),
                (pot_hbm, pot),
                (kern_hbm, kern),
                (first_hbm, first),
                (firstt_hbm, firstt),
                (second_hbm, second),
            )
        )
    ]
    for load in loads:
        load.start()

    def around(place, j):
        return lax.rem(place + offset(j), 8)

    barrier = pltpu.get_barrier_semaphore()

    def greet(step, _):
        peer = around(row, step // 8) * 8 + around(col, step % 8)
        pl.semaphore_signal(barrier, inc=1, device_id={"band": peer}, device_id_type=MESH)
        return 0

    lax.fori_loop(0, 63, greet, 0)

    def greet_kpt(step, _):
        pl.semaphore_signal(
            barrier, inc=1, device_id={"kpt": lax.rem(mine + step, 8)}, device_id_type=MESH
        )
        return 0

    lax.fori_loop(1, 8, greet_kpt, 0)

    loads[0].wait()

    def pack(d, _):
        block = x[:, :, pl.ds(pl.multiple_of(d * 512, 512), 512)]
        wide = block.astype(F32).reshape(8, 512)
        for i in range(4):
            spread[pl.ds(pl.multiple_of(d * 8, 8) + i * 512, 8), :] = wide[
                :, i * 128 : (i + 1) * 128
            ]
        osend[d] = wide.astype(BF16)
        return 0

    lax.fori_loop(0, 64, pack, 0)
    pl.semaphore_wait(barrier, 70)

    def send(source, target, peer, n, arrival):
        pltpu.make_async_remote_copy(
            src_ref=source,
            dst_ref=target,
            send_sem=ssem.at[n],
            recv_sem=arrival,
            device_id={"band": peer},
            device_id_type=MESH,
        ).start()

    def wait(sem, dst, count):
        part = dst.at[pl.ds(0, count)]
        pltpu.make_async_copy(part, part, sem).wait()

    def to_all(n, source, dst, arrival):
        def go(step, _):
            peer = around(row, step // 8) * 8 + around(col, step % 8)
            send(source(peer), dst.at[me], peer, n, arrival(step // 8))
            return 0

        lax.fori_loop(0, 63, go, 0)

    def to_row(n, base, count, source, dst, arrival):
        def go(j, _):
            peer = base + around(col, j)
            send(source(peer), dst.at[me], peer, n, arrival)
            return 0

        lax.fori_loop(0, count, go, 0)

    def by_rows(step):
        def run(g, _):
            step(g, 8)
            return 0

        lax.fori_loop(0, 7, run, 0)
        step(7, 7)

    orecv[me] = osend[me]
    to_all(0, lambda p: osend.at[p], orecv, lambda g: rsem.at[0])

    for f in range(8):
        for r in range(8):
            for i in range(4):
                at = r * 32 + i * 8
                bands[f, at : at + 8, :] = spread[pl.ds(i * 512 + r * 64 + f, 8, stride=8), :]
    loads[2].wait()
    lane128 = lax.broadcasted_iota(jnp.int32, (32, 128), 1)
    for h in range(8):
        tile = jnp.zeros((32, 128), F32)
        for j in range(4):
            piece = kern[pl.ds(2 * j + h // 4, 32, stride=8), :]
            shift = (j * 32 - (h % 4) * 32) % 128
            if shift:
                piece = pltpu.roll(piece, shift, 1)
            tile = jnp.where(lane128 // 32 == j, piece, tile)
        kgrid[h] = tile * (1.0 / (GRID * SCALE**4))

    wait(rsem.at[0], orecv, 63)
    xs[...] = orecv[...].astype(F32).reshape(512, 512).astype(BF16)

    line = lax.broadcasted_iota(jnp.int32, (8, 512), 0)
    place = lax.broadcasted_iota(jnp.int32, (8, 512), 1)
    want = jnp.zeros((8, 512), jnp.int32)
    for o in range(OWNERS):
        band = owners[o]
        base = (band // 4) * 8 + band % 4
        want = jnp.where(line // 2 == o, base + (line % 2) * 4, want)
    pick = jnp.where(place == want, 1.0, 0.0).astype(BF16)
    share = jnp.dot(pick, xs[...], preferred_element_type=F32).astype(BF16)
    sh[mine] = share

    def kpt_go(step, _):
        pltpu.make_async_remote_copy(
            src_ref=sh.at[mine],
            dst_ref=sh.at[mine],
            send_sem=ssem.at[1],
            recv_sem=rsem.at[1],
            device_id={"kpt": lax.rem(mine + step, 8)},
            device_id_type=MESH,
        ).start()
        return 0

    lax.fori_loop(1, 8, kpt_go, 0)

    def fold(gram):
        rows = gram.shape[0]
        half = lax.broadcasted_iota(jnp.int32, gram.shape, 1) % 8 < 4
        low = pltpu.roll(gram, rows - 4, 0)
        swapped = jnp.where(half, pltpu.roll(low, 508, 1), -pltpu.roll(low, 4, 1))
        sums = ((gram + swapped) * (1.0 / GRID)).reshape(rows // 8, 8, 512)[:, :4, :]
        return sums.reshape(rows // 2, 512)

    def widen(flat):
        half = lax.broadcasted_iota(jnp.int32, flat.shape, 1) % 8 < 4
        other = jnp.where(half, -pltpu.roll(flat, 508, 1), pltpu.roll(flat, 4, 1))
        count = flat.shape[0] // 4
        both = [flat.reshape(count, 4, 512), other.reshape(count, 4, 512)]
        return jnp.concatenate(both, axis=1).reshape(count * 8, 512)

    def ahead(shape, base):
        line = lax.broadcasted_iota(jnp.int32, shape, 0)
        lane = lax.broadcasted_iota(jnp.int32, shape, 1)
        return lane - (base + line // 4) * 8 - line % 4

    def halve(flat, base):
        high = flat.astype(BF16).astype(F32)
        rest = pltpu.roll(flat - high, 4, 1)
        return jnp.where(ahead(flat.shape, base) == 4, rest, high).astype(BF16)

    def join(flat, base):
        at = ahead(flat.shape, base)
        whole = flat + pltpu.roll(flat, 508, 1)
        return jnp.where(at == 0, whole, jnp.where(at == 4, 0.0, flat))

    def gram_of(rows):
        return lax.dot_general(
            rows, xs[...], (((1,), (1,)), ((), ())), preferred_element_type=F32
        )

    msend[...] = halve(fold(gram_of(xs[...])), 0).reshape(64, 4, 512)

    wait(rsem.at[1], sh, 7)
    wanted = jnp.zeros((8, 512), jnp.int32)
    for o in range(OWNERS):
        wanted = jnp.where(line // 2 == o, partner[o, mine], wanted)
    got = jnp.zeros((8, 512), F32)
    for k in range(8):
        got = jnp.where(wanted == k, sh[k].astype(F32), got)

    turned = col * 8 + row
    ph_a[me] = got[:, :256].astype(BF16)
    ph_b[turned] = got[:, 256:].astype(BF16)

    def spread_one(j, _):
        send(ph_a.at[me], ph_a.at[me], row * 8 + around(col, j), 2, asem.at[0, j])
        send(ph_b.at[turned], ph_b.at[turned], around(row, j) * 8 + col, 10, asem.at[1, j])
        return 0

    lax.fori_loop(0, 7, spread_one, 0)

    def pass_on(slot_a, slot_b):
        def go(j, _):
            send(ph_a.at[slot_a], ph_a.at[slot_a], around(row, j) * 8 + col, 3, rsem.at[4])
            send(ph_b.at[slot_b], ph_b.at[slot_b], row * 8 + around(col, j), 11, rsem.at[5])
            return 0

        lax.fori_loop(0, 7, go, 0)

    pass_on(me, turned)

    def relay(i, _):
        j = 6 - i
        wait(asem.at[0, j], ph_a, 1)
        wait(asem.at[1, j], ph_b, 1)
        from_col = lax.rem(col - offset(j) + 8, 8)
        from_row = lax.rem(row - offset(j) + 8, 8)
        pass_on(row * 8 + from_col, col * 8 + from_row)
        return 0

    lax.fori_loop(0, 7, relay, 0)

    mrecv[me] = msend[me]
    to_all(4, lambda p: msend.at[p], mrecv, lambda g: rsem.at[6])

    wait(rsem.at[4], ph_a, 56)
    wait(rsem.at[5], ph_b, 56)
    for i in range(4):
        source = ph_a if i < 2 else ph_b
        at = slice((i % 2) * 128, (i % 2 + 1) * 128)
        spread[i * 512 : (i + 1) * 512, :] = source[:, :, at].astype(F32).reshape(512, 128)

    for f in range(8):
        for r in range(8):
            for i in range(4):
                at = r * 32 + i * 8
                if i < 2:
                    part = spread[pl.ds(i * 512 + r * 64 + f, 8, stride=8), :]
                else:
                    part = spread[pl.ds(i * 512 + r * 8 + f, 8, stride=64), :]
                phases[f, at : at + 8, :] = part

    for load in loads[3:]:
        load.wait()
    for o in range(OWNERS):
        ph_re, ph_im = phases[2 * o], phases[2 * o + 1]
        for b in range(4):
            b_re, b_im = bands[b], bands[4 + b]
            at = b * 128
            dens[0:256, at : at + 128] = (ph_re * b_re + ph_im * b_im).astype(BF16)
            dens[256:512, at : at + 128] = (ph_re * b_im - ph_im * b_re).astype(BF16)
        mid[:, o * 512 : (o + 1) * 512] = jnp.dot(
            first[...], dens[...], preferred_element_type=F32
        ).astype(BF16)

    def inner(h, _):
        r = pl.multiple_of(h * 32, 32)
        rows = jnp.concatenate(
            [
                jnp.concatenate(
                    [
                        mid[pl.ds(r + 256 * c, 32), f * 128 : (f + 1) * 128]
                        for c in range(2)
                    ],
                    axis=1,
                )
                for f in range(16)
            ],
            axis=0,
        )
        spectrum = jnp.dot(rows, second[h], preferred_element_type=F32)
        factor = jnp.concatenate([kgrid[h], kgrid[h]], axis=1)
        spectrum = (spectrum.reshape(16, 32, 256) * factor[None]).reshape(512, 256).astype(BF16)
        back = lax.dot_general(
            spectrum, second[h], (((1,), (1,)), ((), ())), preferred_element_type=F32
        ).astype(BF16)
        for f in range(16):
            for c in range(2):
                mid[pl.ds(r + 256 * c, 32), f * 128 : (f + 1) * 128] = back[
                    f * 32 : (f + 1) * 32, c * 128 : (c + 1) * 128
                ]
        return 0

    lax.fori_loop(0, 8, inner, 0)

    wait(rsem.at[6], mrecv, 63)
    margin = join(jnp.sum(mrecv[...].astype(F32), axis=0), me)
    whole = halve(margin, me)
    m_a[me] = whole[:, :256]
    m_b[turned] = whole[:, 256:]

    def margin_one(j, _):
        send(m_a.at[me], m_a.at[me], row * 8 + around(col, j), 5, rsem.at[2])
        send(m_b.at[turned], m_b.at[turned], around(row, j) * 8 + col, 12, rsem.at[3])
        return 0

    lax.fori_loop(0, 7, margin_one, 0)

    def margin_all(j, _):
        part_a = m_a.at[pl.ds(row * 8, 8)]
        part_b = m_b.at[pl.ds(col * 8, 8)]
        send(part_a, part_a, around(row, j) * 8 + col, 13, rsem.at[7])
        send(part_b, part_b, row * 8 + around(col, j), 14, rsem.at[9])
        return 0

    loads[1].wait()

    def values_out(g, count):
        r = around(row, g)
        base = pl.multiple_of(r * 32, 32)
        local = jnp.concatenate(
            [pot[pl.ds(r * 32 + i, 8, stride=4), :] for i in range(4)], axis=0
        )
        slot = pl.multiple_of(lax.rem(g, 4) * 32, 32)
        for f in range(8):
            value = local * bands[f, pl.ds(base, 32), :] + SHARE * acc[f, pl.ds(slot, 32), :]
            for i in range(4):
                spread[pl.ds(i * 512 + r * 64 + f, 8, stride=8), :] = value[i * 8 : (i + 1) * 8]
        first_slab = pl.multiple_of(r * 8, 8)
        for i in range(4):
            part = spread[pl.ds(pl.multiple_of(i * 512 + r * 64, 64), 64), :]
            vsend[pl.ds(first_slab, 8), :, i * 128 : (i + 1) * 128] = part.reshape(
                8, 8, 128
            ).astype(BF16)
        to_row(6, first_slab, count, lambda p: vsend.at[p], vrecv, gsem.at[0, g])

    for half in range(2):
        starts = [
            pl.multiple_of(around(row, 4 * half + q) * 32, 32) for q in range(4)
        ]

        def chosen(ref, at=0):
            return jnp.concatenate([ref[pl.ds(at + r, 32), :] for r in starts], axis=0)

        lines = jnp.concatenate([chosen(firstt), chosen(firstt, 256)], axis=0)
        for o in range(OWNERS):
            if half == 0 and o == 3:
                wait(rsem.at[2], m_a, 7)
                wait(rsem.at[3], m_b, 7)
                lax.fori_loop(0, 7, margin_all, 0)
            ph_re, ph_im = chosen(phases.at[2 * o]), chosen(phases.at[2 * o + 1])
            solved = jnp.dot(
                lines, mid[:, o * 512 : (o + 1) * 512], preferred_element_type=F32
            )
            for b in range(4):
                s_re = solved[0:128, b * 128 : (b + 1) * 128]
                s_im = solved[128:256, b * 128 : (b + 1) * 128]
                t_re = ph_re * s_re - ph_im * s_im
                t_im = ph_re * s_im + ph_im * s_re
                if o:
                    t_re = acc[b] + t_re
                    t_im = acc[4 + b] + t_im
                acc[b] = t_re
                acc[4 + b] = t_im

        def run(g, _):
            values_out(g, 8)
            return 0

        lax.fori_loop(4 * half, 4 + 3 * half, run, 0)
    values_out(7, 7)
    vrecv[me] = vsend[me]

    wait(rsem.at[7], m_a, 56)
    wait(rsem.at[9], m_b, 56)

    def gathered(i, _):
        mall[i, :, 0:256] = m_a[i]
        mall[i, :, 256:512] = m_b[lax.rem(i, 8) * 8 + i // 8]
        return 0

    lax.fori_loop(0, 64, gathered, 0)
    mt[...] = widen(join(mall[...].astype(F32).reshape(256, 512), 0))

    def take_values(g, count):
        source = lax.rem(row - offset(g) + 8, 8)
        base = pl.multiple_of(source * 8, 8)
        wait(gsem.at[0, g], vrecv, count)
        rows = vrecv[pl.ds(base, 8)].astype(F32).reshape(64, 512).astype(BF16)
        ys[pl.ds(pl.multiple_of(source * 64, 64), 64), :] = rows
        psend[pl.ds(base, 8)] = halve(fold(gram_of(rows)), base).reshape(8, 4, 512)
        to_row(7, base, count, lambda p: psend.at[p], precv, rsem.at[8])

    by_rows(take_values)
    precv[me] = psend[me]
    wait(rsem.at[8], precv, 63)
    proj = join(jnp.sum(precv[...].astype(F32), axis=0), me)
    coeff = 2.0 * proj - jnp.dot(
        proj, mt[...], precision=lax.Precision.HIGHEST, preferred_element_type=F32
    )
    cown[...] = coeff.astype(BF16)
    call[me] = cown[...]
    to_all(8, lambda p: cown, call, lambda g: gsem.at[1, g])

    def take_coefficients(g, count):
        source = lax.rem(row - offset(g) + 8, 8)
        base = pl.multiple_of(source * 8, 8)
        wait(gsem.at[1, g], call, count)
        mixing = widen(call[pl.ds(base, 8)].astype(F32).reshape(32, 512)).astype(BF16)
        correction = jnp.dot(mixing, xs[...], preferred_element_type=F32)
        own = ys[pl.ds(pl.multiple_of(source * 64, 64), 64), :].astype(F32)
        rsend[pl.ds(base, 8)] = (own - correction).reshape(8, 8, 512).astype(BF16)
        to_row(9, base, count, lambda p: rsend.at[p], rrecv, gsem.at[2, g])

    by_rows(take_coefficients)
    rrecv[me] = rsend[me]

    def take_residuals(g, count):
        source = around(row, g)
        wait(gsem.at[2, g], rrecv, count)
        base = pl.multiple_of(source * 4096, 4096)
        for s in range(8):
            wide = rrecv[source * 8 + s].astype(F32).reshape(2, 4, 512)
            result[:, :, pl.ds(base + s * 512, 512)] = wide.astype(BF16)
        cells = pl.ds(base, 4096)
        pltpu.make_async_copy(result.at[:, :, cells], out.at[:, :, cells], fsem).start()

    by_rows(take_residuals)
    pltpu.make_async_copy(result, out, fsem).wait()

    for n, ref in (
        (0, osend), (4, msend), (6, vsend), (7, psend), (8, call), (9, rsend)
    ):
        wait(ssem.at[n], ref, 63)
    wait(ssem.at[1], sh, 7)
    for n, ref in ((2, ph_a), (10, ph_b), (5, m_a), (12, m_b)):
        wait(ssem.at[n], ref, 7)
    for n, ref in ((3, ph_a), (11, ph_b), (13, m_a), (14, m_b)):
        wait(ssem.at[n], ref, 56)


def body(orbitals, potential, kernel_grid, owners, partner):
    first, firstt, second = tables()
    smem = pl.BlockSpec(memory_space=pltpu.SMEM)
    anywhere = pl.BlockSpec(memory_space=pl.ANY)
    slab = (64, 8, 512)
    thin = (64, 4, 512)
    out = pl.pallas_call(
        kernel,
        out_shape=jax.ShapeDtypeStruct((2, 4, GRID), BF16),
        in_specs=[anywhere, anywhere, anywhere, smem, smem, anywhere, anywhere, anywhere],
        out_specs=anywhere,
        scratch_shapes=[
            pltpu.VMEM((2, 4, GRID), BF16),
            pltpu.VMEM((256, 128), F32),
            pltpu.VMEM((256, 128), F32),
            pltpu.VMEM((512, 512), BF16),
            pltpu.VMEM((512, 512), BF16),
            pltpu.VMEM((8, 256, 256), BF16),
            pltpu.VMEM((2048, 128), F32),
            pltpu.VMEM((8, 256, 128), F32),
            pltpu.VMEM((8, 32, 128), F32),
            pltpu.VMEM(slab, BF16),
            pltpu.VMEM(slab, BF16),
            pltpu.VMEM((512, 512), BF16),
            pltpu.VMEM((8, 8, 512), BF16),
            pltpu.VMEM((64, 8, 256), BF16),
            pltpu.VMEM((64, 8, 256), BF16),
            pltpu.VMEM(thin, BF16),
            pltpu.VMEM(thin, BF16),
            pltpu.VMEM((64, 4, 256), BF16),
            pltpu.VMEM((64, 4, 256), BF16),
            pltpu.VMEM(thin, BF16),
            pltpu.VMEM((512, 512), F32),
            pltpu.VMEM((512, 512), BF16),
            pltpu.VMEM((512, 2048), BF16),
            pltpu.VMEM((8, 128, 128), F32),
            pltpu.VMEM((8, 256, 128), F32),
            pltpu.VMEM(slab, BF16),
            pltpu.VMEM(slab, BF16),
            pltpu.VMEM((512, 512), BF16),
            pltpu.VMEM(thin, BF16),
            pltpu.VMEM(thin, BF16),
            pltpu.VMEM((4, 512), BF16),
            pltpu.VMEM(thin, BF16),
            pltpu.VMEM(slab, BF16),
            pltpu.VMEM(slab, BF16),
            pltpu.VMEM((2, 4, GRID), BF16),
            pltpu.SemaphoreType.DMA((6,)),
            pltpu.SemaphoreType.DMA((15,)),
            pltpu.SemaphoreType.DMA((10,)),
            pltpu.SemaphoreType.DMA((3, 8)),
            pltpu.SemaphoreType.DMA,
            pltpu.SemaphoreType.DMA((2, 7)),
        ],
        compiler_params=pltpu.CompilerParams(
            collective_id=0, has_side_effects=True, vmem_limit_bytes=60 << 20
        ),
        name="exchange_residual",
    )(
        orbitals[0],
        potential.reshape(256, 128),
        kernel_grid.reshape(256, 128),
        owners,
        partner.T,
        first,
        firstt,
        second,
    )
    return out[None]


def solution(mesh):
    in_specs = (P("kpt", None, "band", None), P(), P("kpt", None), P(), P())
    out_specs = P("kpt", None, "band", None)
    return jax.shard_map(body, mesh=mesh, in_specs=in_specs, out_specs=out_specs, check_vma=False)
```

```python
import jax
import jax.numpy as jnp
import numpy as np
from jax import lax
from jax.experimental import pallas as pl
from jax.experimental.pallas import tpu as pltpu
from jax.sharding import PartitionSpec as P

GRID = 32768
OWNERS = 4
SHARE = -0.25
SCALE = 1.6245
MESH = pl.DeviceIdType.MESH
F32 = jnp.float32
BF16 = jnp.bfloat16


def as_real(m):
    return np.block([[m.real, -m.imag], [m.imag, m.real]])


def tables():
    spot = np.arange(256)
    plane = (spot // 32 * 8 + spot % 8) * 4 + spot // 8 % 4
    cell_x, cell_y = plane // 8, plane % 8
    freq_x, freq_y = spot % 32, spot // 32
    outer = np.exp(
        -2j * np.pi * (freq_x[:, None] * cell_x / 32 + freq_y[:, None] * cell_y / 8)
    )
    lane = np.arange(128)
    high, last = lane // 32, lane % 32
    inner = [
        np.exp(
            -2j
            * np.pi
            * ((h + 8 * high[:, None]) * high / 32 + last[:, None] * last / 32)
        )
        for h in range(8)
    ]
    first = (SCALE * as_real(outer)).astype(BF16)
    second = np.stack([(SCALE * as_real(m).T) for m in inner]).astype(BF16)
    return first, np.ascontiguousarray(first.T), second


def offset(j):
    return 4 + ((j + 1) // 2) * (1 - 2 * (j % 2))


def kernel(
    x_hbm, pot_hbm, kern_hbm, owners, partner, first_hbm, firstt_hbm, second_hbm,
    out,
    x, pot, kern, first, firstt, second, spread, bands, kgrid,
    osend, orecv, xs, sh, ph_a, ph_b, msend, mrecv, m_a, m_b, mall, mt,
    dens, mid, acc, phases, vsend, vrecv, ys, psend, precv, cown, call, rsend, rrecv, result,
    csem, ssem, rsem, gsem, fsem, asem,
):
    me = lax.axis_index("band")
    mine = lax.axis_index("kpt")
    row, col = me // 8, me % 8

    loads = [
        pltpu.make_async_copy(src, dst, csem.at[i])
        for i, (src, dst) in enumerate(
            (
                (x_hbm, x),
                (pot_hbm, pot),
                (kern_hbm, kern),
                (first_hbm, first),
                (firstt_hbm, firstt),
                (second_hbm, second),
            )
        )
    ]
    for load in loads:
        load.start()

    def around(place, j):
        return lax.rem(place + offset(j), 8)

    barrier = pltpu.get_barrier_semaphore()

    rows = [around(row, j) for j in range(8)]
    cols = [around(col, j) for j in range(8)]

    def over_rows(step):
        def run(g, _):
            step(g, around(row, g) * 8, 8)
            return 0

        lax.fori_loop(0, 7, run, 0)
        step(7, row * 8, 7)

    def greet(g, base, count):
        for j in range(count):
            pl.semaphore_signal(
                barrier, inc=1, device_id={"band": base + cols[j]}, device_id_type=MESH
            )

    over_rows(greet)

    def greet_kpt(step, _):
        pl.semaphore_signal(
            barrier, inc=1, device_id={"kpt": lax.rem(mine + step, 8)}, device_id_type=MESH
        )
        return 0

    lax.fori_loop(1, 8, greet_kpt, 0)

    loads[0].wait()

    def pack(d, _):
        block = x[:, :, pl.ds(pl.multiple_of(d * 512, 512), 512)]
        wide = block.astype(F32).reshape(8, 512)
        for i in range(4):
            spread[pl.ds(pl.multiple_of(d * 8, 8) + i * 512, 8), :] = wide[
                :, i * 128 : (i + 1) * 128
            ]
        osend[d] = wide.astype(BF16)
        return 0

    lax.fori_loop(0, 64, pack, 0, unroll=4)
    pl.semaphore_wait(barrier, 70)

    def send(source, target, peer, n, arrival):
        pltpu.make_async_remote_copy(
            src_ref=source,
            dst_ref=target,
            send_sem=ssem.at[n],
            recv_sem=arrival,
            device_id={"band": peer},
            device_id_type=MESH,
        ).start()

    def wait(sem, dst, count):
        part = dst.at[pl.ds(0, count)]
        pltpu.make_async_copy(part, part, sem).wait()

    def to_all(n, source, dst, arrival):
        over_rows(lambda g, base, count: to_row(n, base, count, source, dst, arrival(g)))

    def to_row(n, base, count, source, dst, arrival):
        for j in range(count):
            peer = base + cols[j]
            send(source(peer), dst.at[me], peer, n, arrival)

    def by_rows(step):
        def run(g, _):
            step(g, 8)
            return 0

        lax.fori_loop(0, 7, run, 0)
        step(7, 7)

    orecv[me] = osend[me]
    to_all(0, lambda p: osend.at[p], orecv, lambda g: rsem.at[0])

    for f in range(8):
        for r in range(8):
            for i in range(4):
                at = r * 32 + i * 8
                bands[f, at : at + 8, :] = spread[pl.ds(i * 512 + r * 64 + f, 8, stride=8), :]
    loads[2].wait()
    lane128 = lax.broadcasted_iota(jnp.int32, (32, 128), 1)
    for h in range(8):
        tile = jnp.zeros((32, 128), F32)
        for j in range(4):
            piece = kern[pl.ds(2 * j + h // 4, 32, stride=8), :]
            shift = (j * 32 - (h % 4) * 32) % 128
            if shift:
                piece = pltpu.roll(piece, shift, 1)
            tile = jnp.where(lane128 // 32 == j, piece, tile)
        kgrid[h] = tile * (1.0 / (GRID * SCALE**4))

    wait(rsem.at[0], orecv, 63)
    xs[...] = orecv[...].astype(F32).reshape(512, 512).astype(BF16)

    line = lax.broadcasted_iota(jnp.int32, (8, 512), 0)
    place = lax.broadcasted_iota(jnp.int32, (8, 512), 1)
    want = jnp.zeros((8, 512), jnp.int32)
    for o in range(OWNERS):
        band = owners[o]
        base = (band // 4) * 8 + band % 4
        want = jnp.where(line // 2 == o, base + (line % 2) * 4, want)
    pick = jnp.where(place == want, 1.0, 0.0).astype(BF16)
    share = jnp.dot(pick, xs[...], preferred_element_type=F32).astype(BF16)
    sh[mine] = share

    def kpt_go(step, _):
        pltpu.make_async_remote_copy(
            src_ref=sh.at[mine],
            dst_ref=sh.at[mine],
            send_sem=ssem.at[1],
            recv_sem=rsem.at[1],
            device_id={"kpt": lax.rem(mine + step, 8)},
            device_id_type=MESH,
        ).start()
        return 0

    lax.fori_loop(1, 8, kpt_go, 0)

    def fold(gram):
        height = gram.shape[0]
        half = lax.broadcasted_iota(jnp.int32, gram.shape, 1) % 8 < 4
        low = pltpu.roll(gram, height - 4, 0)
        swapped = jnp.where(half, pltpu.roll(low, 508, 1), -pltpu.roll(low, 4, 1))
        sums = ((gram + swapped) * (1.0 / GRID)).reshape(height // 8, 8, 512)[:, :4, :]
        return sums.reshape(height // 2, 512)

    def widen(flat):
        half = lax.broadcasted_iota(jnp.int32, flat.shape, 1) % 8 < 4
        other = jnp.where(half, -pltpu.roll(flat, 508, 1), pltpu.roll(flat, 4, 1))
        count = flat.shape[0] // 4
        both = [flat.reshape(count, 4, 512), other.reshape(count, 4, 512)]
        return jnp.concatenate(both, axis=1).reshape(count * 8, 512)

    def ahead(shape, base):
        line = lax.broadcasted_iota(jnp.int32, shape, 0)
        lane = lax.broadcasted_iota(jnp.int32, shape, 1)
        return lane - (base + line // 4) * 8 - line % 4

    def halve(flat, base):
        high = flat.astype(BF16).astype(F32)
        rest = pltpu.roll(flat - high, 4, 1)
        return jnp.where(ahead(flat.shape, base) == 4, rest, high).astype(BF16)

    def join(flat, base):
        at = ahead(flat.shape, base)
        whole = flat + pltpu.roll(flat, 508, 1)
        return jnp.where(at == 0, whole, jnp.where(at == 4, 0.0, flat))

    def gram_of(rows):
        return lax.dot_general(
            rows, xs[...], (((1,), (1,)), ((), ())), preferred_element_type=F32
        )

    msend[...] = halve(fold(gram_of(xs[...])), 0).reshape(64, 4, 512)

    wait(rsem.at[1], sh, 7)
    wanted = jnp.zeros((8, 512), jnp.int32)
    for o in range(OWNERS):
        wanted = jnp.where(line // 2 == o, partner[o, mine], wanted)
    got = jnp.zeros((8, 512), F32)
    for k in range(8):
        got = jnp.where(wanted == k, sh[k].astype(F32), got)

    turned = col * 8 + row
    ph_a[me] = got[:, :256].astype(BF16)
    ph_b[turned] = got[:, 256:].astype(BF16)

    for j in range(7):
        send(ph_a.at[me], ph_a.at[me], row * 8 + cols[j], 2, asem.at[0, j])
        send(ph_b.at[turned], ph_b.at[turned], rows[j] * 8 + col, 10, asem.at[1, j])

    def pass_on(slot_a, slot_b):
        for j in range(7):
            send(ph_a.at[slot_a], ph_a.at[slot_a], rows[j] * 8 + col, 3, rsem.at[4])
            send(ph_b.at[slot_b], ph_b.at[slot_b], row * 8 + cols[j], 11, rsem.at[5])

    pass_on(me, turned)

    def relay(i, _):
        j = 6 - i
        wait(asem.at[0, j], ph_a, 1)
        wait(asem.at[1, j], ph_b, 1)
        from_col = lax.rem(col - offset(j) + 8, 8)
        from_row = lax.rem(row - offset(j) + 8, 8)
        pass_on(row * 8 + from_col, col * 8 + from_row)
        return 0

    lax.fori_loop(0, 7, relay, 0)

    mrecv[me] = msend[me]
    to_all(4, lambda p: msend.at[p], mrecv, lambda g: rsem.at[6])

    wait(rsem.at[4], ph_a, 56)
    wait(rsem.at[5], ph_b, 56)
    for i in range(4):
        source = ph_a if i < 2 else ph_b
        at = slice((i % 2) * 128, (i % 2 + 1) * 128)
        spread[i * 512 : (i + 1) * 512, :] = source[:, :, at].astype(F32).reshape(512, 128)

    for f in range(8):
        for r in range(8):
            for i in range(4):
                at = r * 32 + i * 8
                if i < 2:
                    part = spread[pl.ds(i * 512 + r * 64 + f, 8, stride=8), :]
                else:
                    part = spread[pl.ds(i * 512 + r * 8 + f, 8, stride=64), :]
                phases[f, at : at + 8, :] = part

    for load in loads[3:]:
        load.wait()
    for o in range(OWNERS):
        ph_re, ph_im = phases[2 * o], phases[2 * o + 1]
        for b in range(4):
            b_re, b_im = bands[b], bands[4 + b]
            at = b * 128
            dens[0:256, at : at + 128] = (ph_re * b_re + ph_im * b_im).astype(BF16)
            dens[256:512, at : at + 128] = (ph_re * b_im - ph_im * b_re).astype(BF16)
        mid[:, o * 512 : (o + 1) * 512] = jnp.dot(
            first[...], dens[...], preferred_element_type=F32
        ).astype(BF16)

    def inner(h, _):
        r = pl.multiple_of(h * 32, 32)
        rows = jnp.concatenate(
            [
                jnp.concatenate(
                    [
                        mid[pl.ds(r + 256 * c, 32), f * 128 : (f + 1) * 128]
                        for c in range(2)
                    ],
                    axis=1,
                )
                for f in range(16)
            ],
            axis=0,
        )
        spectrum = jnp.dot(rows, second[h], preferred_element_type=F32)
        factor = jnp.concatenate([kgrid[h], kgrid[h]], axis=1)
        spectrum = (spectrum.reshape(16, 32, 256) * factor[None]).reshape(512, 256).astype(BF16)
        back = lax.dot_general(
            spectrum, second[h], (((1,), (1,)), ((), ())), preferred_element_type=F32
        ).astype(BF16)
        for f in range(16):
            for c in range(2):
                mid[pl.ds(r + 256 * c, 32), f * 128 : (f + 1) * 128] = back[
                    f * 32 : (f + 1) * 32, c * 128 : (c + 1) * 128
                ]
        return 0

    lax.fori_loop(0, 8, inner, 0)

    wait(rsem.at[6], mrecv, 63)
    margin = join(jnp.sum(mrecv[...].astype(F32), axis=0), me)
    whole = halve(margin, me)
    m_a[me] = whole[:, :256]
    m_b[turned] = whole[:, 256:]

    for j in range(7):
        send(m_a.at[me], m_a.at[me], row * 8 + cols[j], 5, rsem.at[2])
        send(m_b.at[turned], m_b.at[turned], rows[j] * 8 + col, 12, rsem.at[3])

    def margin_all():
        part_a = m_a.at[pl.ds(row * 8, 8)]
        part_b = m_b.at[pl.ds(col * 8, 8)]
        for j in range(7):
            send(part_a, part_a, rows[j] * 8 + col, 13, rsem.at[7])
            send(part_b, part_b, row * 8 + cols[j], 14, rsem.at[9])

    loads[1].wait()

    def values_out(g, count):
        r = around(row, g)
        base = pl.multiple_of(r * 32, 32)
        local = jnp.concatenate(
            [pot[pl.ds(r * 32 + i, 8, stride=4), :] for i in range(4)], axis=0
        )
        slot = pl.multiple_of(lax.rem(g, 4) * 32, 32)
        for f in range(8):
            value = local * bands[f, pl.ds(base, 32), :] + SHARE * acc[f, pl.ds(slot, 32), :]
            for i in range(4):
                spread[pl.ds(i * 512 + r * 64 + f, 8, stride=8), :] = value[i * 8 : (i + 1) * 8]
        first_slab = pl.multiple_of(r * 8, 8)
        for i in range(4):
            part = spread[pl.ds(pl.multiple_of(i * 512 + r * 64, 64), 64), :]
            vsend[pl.ds(first_slab, 8), :, i * 128 : (i + 1) * 128] = part.reshape(
                8, 8, 128
            ).astype(BF16)
        to_row(6, first_slab, count, lambda p: vsend.at[p], vrecv, gsem.at[0, g])

    for half in range(2):
        starts = [
            pl.multiple_of(around(row, 4 * half + q) * 32, 32) for q in range(4)
        ]

        def chosen(ref, at=0):
            return jnp.concatenate([ref[pl.ds(at + r, 32), :] for r in starts], axis=0)

        lines = jnp.concatenate([chosen(firstt), chosen(firstt, 256)], axis=0)
        for o in range(OWNERS):
            if half == 0 and o == 3:
                wait(rsem.at[2], m_a, 7)
                wait(rsem.at[3], m_b, 7)
                margin_all()
            ph_re, ph_im = chosen(phases.at[2 * o]), chosen(phases.at[2 * o + 1])
            solved = jnp.dot(
                lines, mid[:, o * 512 : (o + 1) * 512], preferred_element_type=F32
            )
            for b in range(4):
                s_re = solved[0:128, b * 128 : (b + 1) * 128]
                s_im = solved[128:256, b * 128 : (b + 1) * 128]
                t_re = ph_re * s_re - ph_im * s_im
                t_im = ph_re * s_im + ph_im * s_re
                if o:
                    t_re = acc[b] + t_re
                    t_im = acc[4 + b] + t_im
                acc[b] = t_re
                acc[4 + b] = t_im

        def run(g, _):
            values_out(g, 8)
            return 0

        lax.fori_loop(4 * half, 4 + 3 * half, run, 0)
    values_out(7, 7)
    vrecv[me] = vsend[me]

    wait(rsem.at[7], m_a, 56)
    wait(rsem.at[9], m_b, 56)

    def gathered(i, _):
        mall[i, :, 0:256] = m_a[i]
        mall[i, :, 256:512] = m_b[lax.rem(i, 8) * 8 + i // 8]
        return 0

    lax.fori_loop(0, 64, gathered, 0)
    mt[...] = widen(join(mall[...].astype(F32).reshape(256, 512), 0))

    def take_values(g, count):
        source = lax.rem(row - offset(g) + 8, 8)
        base = pl.multiple_of(source * 8, 8)
        wait(gsem.at[0, g], vrecv, count)
        rows = vrecv[pl.ds(base, 8)].astype(F32).reshape(64, 512).astype(BF16)
        ys[pl.ds(pl.multiple_of(source * 64, 64), 64), :] = rows
        psend[pl.ds(base, 8)] = halve(fold(gram_of(rows)), base).reshape(8, 4, 512)
        to_row(7, base, count, lambda p: psend.at[p], precv, rsem.at[8])

    by_rows(take_values)
    precv[me] = psend[me]
    wait(rsem.at[8], precv, 63)
    proj = join(jnp.sum(precv[...].astype(F32), axis=0), me)
    coeff = 2.0 * proj - jnp.dot(
        proj, mt[...], precision=lax.Precision.HIGHEST, preferred_element_type=F32
    )
    cown[...] = coeff.astype(BF16)
    call[me] = cown[...]
    to_all(8, lambda p: cown, call, lambda g: gsem.at[1, g])

    def take_coefficients(g, count):
        source = lax.rem(row - offset(g) + 8, 8)
        base = pl.multiple_of(source * 8, 8)
        wait(gsem.at[1, g], call, count)
        mixing = widen(call[pl.ds(base, 8)].astype(F32).reshape(32, 512)).astype(BF16)
        correction = jnp.dot(mixing, xs[...], preferred_element_type=F32)
        own = ys[pl.ds(pl.multiple_of(source * 64, 64), 64), :].astype(F32)
        rsend[pl.ds(base, 8)] = (own - correction).reshape(8, 8, 512).astype(BF16)
        to_row(9, base, count, lambda p: rsend.at[p], rrecv, gsem.at[2, g])

    by_rows(take_coefficients)
    rrecv[me] = rsend[me]

    def take_residuals(g, count):
        source = around(row, g)
        wait(gsem.at[2, g], rrecv, count)
        base = pl.multiple_of(source * 4096, 4096)
        for s in range(8):
            wide = rrecv[source * 8 + s].astype(F32).reshape(2, 4, 512)
            result[:, :, pl.ds(base + s * 512, 512)] = wide.astype(BF16)
        cells = pl.ds(base, 4096)
        pltpu.make_async_copy(result.at[:, :, cells], out.at[:, :, cells], fsem).start()

    by_rows(take_residuals)
    pltpu.make_async_copy(result, out, fsem).wait()

    for n, ref in (
        (0, osend), (4, msend), (6, vsend), (7, psend), (8, call), (9, rsend)
    ):
        wait(ssem.at[n], ref, 63)
    wait(ssem.at[1], sh, 7)
    for n, ref in ((2, ph_a), (10, ph_b), (5, m_a), (12, m_b)):
        wait(ssem.at[n], ref, 7)
    for n, ref in ((3, ph_a), (11, ph_b), (13, m_a), (14, m_b)):
        wait(ssem.at[n], ref, 56)


def body(orbitals, potential, kernel_grid, owners, partner):
    first, firstt, second = tables()
    smem = pl.BlockSpec(memory_space=pltpu.SMEM)
    anywhere = pl.BlockSpec(memory_space=pl.ANY)
    slab = (64, 8, 512)
    thin = (64, 4, 512)
    out = pl.pallas_call(
        kernel,
        out_shape=jax.ShapeDtypeStruct((2, 4, GRID), BF16),
        in_specs=[anywhere, anywhere, anywhere, smem, smem, anywhere, anywhere, anywhere],
        out_specs=anywhere,
        scratch_shapes=[
            pltpu.VMEM((2, 4, GRID), BF16),
            pltpu.VMEM((256, 128), F32),
            pltpu.VMEM((256, 128), F32),
            pltpu.VMEM((512, 512), BF16),
            pltpu.VMEM((512, 512), BF16),
            pltpu.VMEM((8, 256, 256), BF16),
            pltpu.VMEM((2048, 128), F32),
            pltpu.VMEM((8, 256, 128), F32),
            pltpu.VMEM((8, 32, 128), F32),
            pltpu.VMEM(slab, BF16),
            pltpu.VMEM(slab, BF16),
            pltpu.VMEM((512, 512), BF16),
            pltpu.VMEM((8, 8, 512), BF16),
            pltpu.VMEM((64, 8, 256), BF16),
            pltpu.VMEM((64, 8, 256), BF16),
            pltpu.VMEM(thin, BF16),
            pltpu.VMEM(thin, BF16),
            pltpu.VMEM((64, 4, 256), BF16),
            pltpu.VMEM((64, 4, 256), BF16),
            pltpu.VMEM(thin, BF16),
            pltpu.VMEM((512, 512), F32),
            pltpu.VMEM((512, 512), BF16),
            pltpu.VMEM((512, 2048), BF16),
            pltpu.VMEM((8, 128, 128), F32),
            pltpu.VMEM((8, 256, 128), F32),
            pltpu.VMEM(slab, BF16),
            pltpu.VMEM(slab, BF16),
            pltpu.VMEM((512, 512), BF16),
            pltpu.VMEM(thin, BF16),
            pltpu.VMEM(thin, BF16),
            pltpu.VMEM((4, 512), BF16),
            pltpu.VMEM(thin, BF16),
            pltpu.VMEM(slab, BF16),
            pltpu.VMEM(slab, BF16),
            pltpu.VMEM((2, 4, GRID), BF16),
            pltpu.SemaphoreType.DMA((6,)),
            pltpu.SemaphoreType.DMA((15,)),
            pltpu.SemaphoreType.DMA((10,)),
            pltpu.SemaphoreType.DMA((3, 8)),
            pltpu.SemaphoreType.DMA,
            pltpu.SemaphoreType.DMA((2, 7)),
        ],
        compiler_params=pltpu.CompilerParams(
            collective_id=0, has_side_effects=True, vmem_limit_bytes=60 << 20
        ),
        name="exchange_residual",
    )(
        orbitals[0],
        potential.reshape(256, 128),
        kernel_grid.reshape(256, 128),
        owners,
        partner.T,
        first,
        firstt,
        second,
    )
    return out[None]


def solution(mesh):
    in_specs = (P("kpt", None, "band", None), P(), P("kpt", None), P(), P())
    out_specs = P("kpt", None, "band", None)
    return jax.shard_map(body, mesh=mesh, in_specs=in_specs, out_specs=out_specs, check_vma=False)
```
